256 devices in a mesh: sect: 4 (over y), dp: 8 (over x, z_lo), tp: 8 (over z_hi, core).
Axes of the slice: x: 4, y: 4, z: 8 (z_hi: 4, z_lo: 2; z = z_hi * 2 + z_lo), core: 2. Of those that a mesh axis runs over, the one named last changes fastest.
Arguments:
- queries: bfloat16 [8, 64, 48, 128], P('dp', 'sect', 'tp'), may hold values from -250 to 250
- key_cache: bfloat16 [8, 64, 8, 192, 128], P('dp', 'sect', 'tp'), may hold values from -6 to 6
- cached_values: bfloat16 [8, 64, 8, 192, 128], P('dp', 'sect', 'tp'), may hold values from -12 to 12
- incoming_keys: bfloat16 [8, 64, 8, 128], P('dp', 'sect', 'tp'), may hold values from -12 to 12
- incoming_values: bfloat16 [8, 64, 8, 128], P('dp', 'sect', 'tp'), may hold values from -12 to 12
- lengths: int32 [8, 64], P('dp', 'sect'), may hold values from 2 to 192, as said below
- residual: bfloat16 [512, 6144], P('dp', ('sect', 'tp')), may hold values from -8 to 8
- out_proj: bfloat16 [6144, 6144], P(None, ('sect', 'tp')), may hold values from -0.078125 to 0.078125
- norm_gain: float32 [6144], replicated, may hold values from 0.1 to 1.9
- router: bfloat16 [6144, 8], replicated, may hold values from -0.21875 to 0.21875
- gate_proj: bfloat16 [8, 6144, 8192], P('dp', 'sect', 'tp'), may hold values from -0.078125 to 0.078125
- up_proj: bfloat16 [8, 6144, 8192], P('dp', 'sect', 'tp'), may hold values from -0.078125 to 0.078125
- down_proj: bfloat16 [8, 8192, 6144], P('dp', 'tp', 'sect'), may hold values from -0.09375 to 0.09375
- routes: int32 [512, 2], P('dp'), may hold values from 0 to 7, as said below
Outputs:
- mixed: bfloat16 [512, 6144], P('dp', ('sect', 'tp'))
The draws below stay inside these ranges and needn't reach their ends.
Inputs may be any that keep to these rules, and one draw needn't show every extreme that they name: `lengths`: each sequence has 2 or more filled slots; some sequence has all 192 filled. `routes`: the two experts of a token differ. In each block of 64 tokens held by one index of dp, no expert is named by more than 32 tokens, and the same expert is named by exactly 32 tokens in every block.
All inputs are finite; a program needn't handle non-finite values.
Results may differ from the reference program's by a relative error of at most 0.022.
Values may be sent and summed in bfloat16 or wider, within the bound.
No kernel may reach another device: no remote copies, remote signals or barrier semaphores. Data moves between devices by JAX's collectives and lax.ppermute only.
A program may use at most 128 MiB of HBM per device.

```python
import math
import jax
import jax.numpy as jnp
from jax import lax

D = 6144
QUERY_HEADS = 48
KEY_VALUE_HEADS = 8
HEAD_DIM = 128
FFW = 8192
CONTEXT_SLOTS = 192
EXPERTS = 8
GROUP_TOKENS = 64
BATCH = 512
CAP = 32
N_DP = 8


def loguniform_draw(key, shape, lowest, highest):
    return jnp.exp(jax.random.uniform(key, shape, jnp.float32, jnp.log(lowest), jnp.log(highest)))


def attention_pair(key):
    queries = jnp.clip(jax.random.normal(jax.random.fold_in(key, 12), (N_DP, GROUP_TOKENS, QUERY_HEADS, HEAD_DIM), jnp.float32), -6.0, 6.0)
    cached_entries = jnp.clip(jax.random.normal(jax.random.fold_in(key, 11), (N_DP, GROUP_TOKENS, KEY_VALUE_HEADS, CONTEXT_SLOTS, HEAD_DIM), jnp.float32), -6.0, 6.0)
    return (queries, cached_entries)


def draw_queries(key, part):
    return attention_pair(key)[0].astype(jnp.bfloat16)


def draw_key_cache(key, part):
    return attention_pair(key)[1].astype(jnp.bfloat16)


def draw_lengths(key, part):
    drawn_lengths = jax.random.randint(jax.random.fold_in(key, 21), (N_DP * GROUP_TOKENS,), 2, CONTEXT_SLOTS + 1)
    forced_index = jax.random.randint(jax.random.fold_in(key, 22), (), 0, N_DP * GROUP_TOKENS)
    return drawn_lengths.at[forced_index].set(CONTEXT_SLOTS).reshape(N_DP, GROUP_TOKENS)


def draw_residual(key, part):
    entries = jax.random.normal(jax.random.fold_in(key, 41), (BATCH, D), jnp.float32)
    row_scale = loguniform_draw(jax.random.fold_in(key, 42), (BATCH, 1), 0.3, 1.5)
    column_scale = loguniform_draw(jax.random.fold_in(key, 43), (1, D), 0.3, 1.5)
    return jnp.clip(entries * row_scale * column_scale, -8.0, 8.0).astype(jnp.bfloat16)


def draw_routes(key, part):
    busiest = jax.random.randint(jax.random.fold_in(key, 31), (), 0, EXPERTS)
    half_rows = GROUP_TOKENS // 2
    position = jnp.arange(GROUP_TOKENS, dtype=jnp.int32)

    def one_block(block_number):
        block_key = jax.random.fold_in(key, 100 + block_number)
        shuffled = jax.random.permutation(jax.random.fold_in(block_key, 1), GROUP_TOKENS)
        offset = jax.random.randint(jax.random.fold_in(block_key, 2), (), 0, EXPERTS - 1)
        hot_side = jax.random.randint(jax.random.fold_in(block_key, 3), (GROUP_TOKENS,), 0, 2)
        first_slot = jnp.where(position < half_rows, position, half_rows + 2 * (position - half_rows))
        first_other = (offset + first_slot) % (EXPERTS - 1)
        second_other = (offset + first_slot + 1) % (EXPERTS - 1)
        first_other = first_other + (first_other >= busiest).astype(jnp.int32)
        second_other = second_other + (second_other >= busiest).astype(jnp.int32)
        leading = jnp.where(position < half_rows, jnp.where(hot_side == 0, busiest, first_other), first_other)
        trailing = jnp.where(position < half_rows, jnp.where(hot_side == 0, first_other, busiest), second_other)
        route_pair = jnp.stack([leading, trailing], axis=1).astype(jnp.int32)
        return jnp.zeros((GROUP_TOKENS, 2), jnp.int32).at[shuffled].set(route_pair)
    blocks = jax.vmap(one_block)(jnp.arange(N_DP, dtype=jnp.int32))
    return blocks.reshape(BATCH, 2)


def with_spikes(array, key, source, target, parts, factor):
    owner, partner = [(jnp.arange(array.shape[axis_at]) // (array.shape[axis_at] // parts)).reshape([-1 if axis == axis_at else 1 for axis in range(array.ndim)]) for axis_at in (source, target)]
    chosen = jax.random.permutation(key, parts)[partner]
    strong = (owner == chosen) | (owner == (partner + parts // 2) % parts)
    return jnp.where(strong, factor * array, array)


def shard_levels(stream_key, dims, pieces, least, largest):
    def one(dim, shards_of):
        steps = jax.random.uniform(jax.random.fold_in(jax.random.fold_in(stream_key, 6), dim), (shards_of,), jnp.float32, least / len(pieces), largest / len(pieces))
        return jnp.repeat(jnp.exp(steps), dims[dim] // shards_of).reshape((-1,) + (1,) * (len(dims) - dim - 1))

    gain = one(*pieces[0])
    for cut in pieces[1:]:
        gain = gain * one(*cut)
    return gain


def bell_draw(stream_key, shape, scale, reach, split=(), kind=jnp.bfloat16):
    drawn = scale * jax.random.normal(stream_key, shape, jnp.float32)
    if split:
        drawn = drawn * shard_levels(stream_key, shape, split, -0.22, 0.18)
    return jnp.clip(drawn, -reach, reach).astype(kind)


def bell_draw_with(own_key, extent, deviation, reach, shards, heavy, kind=jnp.bfloat16):
    drawn = deviation * jax.random.normal(own_key, extent, jnp.float32)
    if shards:
        drawn = drawn * shard_levels(own_key, extent, shards, -0.22, 0.18)
    return jnp.clip(with_spikes(drawn, jax.random.fold_in(own_key, 3), *heavy), -reach, reach).astype(kind)


def setup_inputs(seed: int = 0) -> dict:
    arg_keys = jax.random.split(jax.random.key(seed), 15)
    queries = draw_queries(jax.random.fold_in(arg_keys[14], 71), 0)
    key_cache = draw_key_cache(jax.random.fold_in(arg_keys[14], 71), 0)
    cached_values = bell_draw(arg_keys[2], (N_DP, GROUP_TOKENS, KEY_VALUE_HEADS, CONTEXT_SLOTS, HEAD_DIM), 2.0, 12.0, ((0, 8), (1, 4), (2, 8)))
    incoming_keys = bell_draw(arg_keys[3], (N_DP, GROUP_TOKENS, KEY_VALUE_HEADS, HEAD_DIM), 2.0, 12.0, ((0, 8), (1, 4), (2, 8)))
    incoming_values = bell_draw(arg_keys[4], (N_DP, GROUP_TOKENS, KEY_VALUE_HEADS, HEAD_DIM), 2.0, 12.0, ((0, 8), (1, 4), (2, 8)))
    lengths = draw_lengths(jax.random.fold_in(arg_keys[14], 71), 0)
    residual = draw_residual(jax.random.fold_in(arg_keys[14], 71), 0)
    out_proj = bell_draw(arg_keys[7], (QUERY_HEADS * HEAD_DIM, D), (QUERY_HEADS * HEAD_DIM) ** -0.5, 0.078125, ((1, 32),))
    norm_gain = jnp.clip(1.0 + 0.18 * jax.random.normal(arg_keys[8], (D,), jnp.float32), 0.1, 1.9)
    router = bell_draw(arg_keys[9], (D, EXPERTS), (D // 9) ** -0.5, 0.21875)
    gate_proj = bell_draw(arg_keys[10], (EXPERTS, D, FFW), D ** -0.5, 0.078125, ((0, 8), (1, 4), (2, 8)))
    up_proj = bell_draw(arg_keys[11], (EXPERTS, D, FFW), D ** -0.5, 0.078125, ((0, 8), (1, 4), (2, 8)))
    down_proj = bell_draw_with(arg_keys[12], (EXPERTS, FFW, D), FFW ** -0.5, 0.09375, ((0, 8), (1, 8), (2, 4)), (1, 2, 8, 2.0))
    routes = draw_routes(jax.random.fold_in(arg_keys[14], 71), 0)
    return dict(queries=queries, key_cache=key_cache, cached_values=cached_values, incoming_keys=incoming_keys, incoming_values=incoming_values, lengths=lengths, residual=residual, out_proj=out_proj, norm_gain=norm_gain, router=router, gate_proj=gate_proj, up_proj=up_proj, down_proj=down_proj, routes=routes)


norm_epsilon = 1e-05

def attend(queries, key_cache, cached_values, incoming_keys, incoming_values, lengths):
    tokens = queries.shape[0]
    query_heads = queries.shape[1]
    head_size = queries.shape[2]
    kv_heads = key_cache.shape[1]
    heads_per_group = query_heads // kv_heads
    logit_scale = 1.0 / math.sqrt(head_size)
    query_head_groups = queries.astype(jnp.float32).reshape(tokens, kv_heads, heads_per_group, head_size)
    cached_entries = jnp.einsum('bkgd,bkpd->bkgp', query_head_groups, key_cache.astype(jnp.float32)) * logit_scale
    new_token_score = jnp.einsum('ncwt,nct->ncw', query_head_groups, incoming_keys.astype(jnp.float32)) * logit_scale
    positions = jnp.arange(key_cache.shape[2], dtype=jnp.int32)
    valid_slots = positions[None, :] < lengths[:, None]
    cached_entries = jnp.where(valid_slots[:, None, None, :], cached_entries, -jnp.inf)
    highest = jnp.maximum(lax.optimization_barrier(jnp.max(cached_entries, axis=-1)), new_token_score)
    cached_exp = jnp.exp(cached_entries - highest[..., None])
    fresh_exp = jnp.exp(new_token_score - highest)
    denominator = lax.optimization_barrier(jnp.sum(cached_exp, axis=-1)) + fresh_exp
    cached_prob = (cached_exp / denominator[..., None]).astype(jnp.bfloat16)
    fresh_prob = (fresh_exp / denominator).astype(jnp.bfloat16)
    gathered = jnp.einsum('bkgp,bkpd->bkgd', cached_prob.astype(jnp.float32), cached_values.astype(jnp.float32))
    gathered = gathered + fresh_prob.astype(jnp.float32)[..., None] * incoming_values.astype(jnp.float32)[:, :, None, :]
    return gathered.reshape(tokens, query_heads * head_size).astype(jnp.bfloat16)

def attend_block(blocks):
    return attend(blocks[0], blocks[1], blocks[2], blocks[3], blocks[4], blocks[5])

def normalize(rows_in, norm_gain):
    values = rows_in.astype(jnp.float32)
    mean_square = lax.optimization_barrier(jnp.mean(values * values, axis=-1, keepdims=True))
    return (values * lax.rsqrt(mean_square + norm_epsilon) * norm_gain).astype(jnp.bfloat16)

def run_expert(packed):
    rows_in, gate_weight, up_weight, down_weight = packed
    gate_pre = jnp.dot(rows_in, gate_weight, preferred_element_type=jnp.float32)
    up_pre = jnp.dot(rows_in, up_weight, preferred_element_type=jnp.float32)
    activated = (jax.nn.silu(gate_pre) * up_pre).astype(jnp.bfloat16)
    return jnp.dot(activated, down_weight, preferred_element_type=jnp.float32).astype(jnp.bfloat16)

def reference(queries, key_cache, cached_values, incoming_keys, incoming_values, lengths, residual, out_proj, norm_gain, router, gate_proj, up_proj, down_proj, routes):
    attended = lax.map(attend_block, (queries, key_cache, cached_values, incoming_keys, incoming_values, lengths))
    attended = attended.reshape(BATCH, QUERY_HEADS * HEAD_DIM)
    projected = jnp.dot(attended, out_proj, preferred_element_type=jnp.float32)
    hidden = (residual.astype(jnp.float32) + projected).astype(jnp.bfloat16)
    normed = normalize(hidden, norm_gain)
    logits = jnp.dot(normed, router, preferred_element_type=jnp.float32)
    chosen = jnp.take_along_axis(logits, routes, axis=1)
    mixing = jax.nn.sigmoid(chosen - chosen[:, ::-1])
    block_routes = routes.reshape(N_DP, 2 * GROUP_TOKENS)
    onehot = (block_routes[..., None] == jnp.arange(EXPERTS, dtype=jnp.int32)[None, None, :]).astype(jnp.int32)
    earlier = jnp.cumsum(onehot, axis=1) - onehot
    target = block_routes * CAP + lax.optimization_barrier(jnp.sum(earlier * onehot, axis=2))
    token_index = jnp.arange(2 * GROUP_TOKENS, dtype=jnp.int32) // 2
    normed_blocks = normed.reshape(N_DP, GROUP_TOKENS, D)

    def fill_block(packed):
        rows_in, slots = packed
        return jnp.zeros((EXPERTS * CAP, D), jnp.bfloat16).at[slots].set(rows_in[token_index])
    buffers = lax.map(fill_block, (normed_blocks, target))
    per_expert = buffers.reshape(N_DP, EXPERTS, CAP, D).transpose(1, 0, 2, 3).reshape(EXPERTS, N_DP * CAP, D)
    outputs = lax.map(run_expert, (per_expert, gate_proj, up_proj, down_proj))
    by_block = outputs.reshape(EXPERTS, N_DP, CAP, D).transpose(1, 0, 2, 3).reshape(N_DP * EXPERTS * CAP, D)
    flat_index = (jnp.arange(N_DP, dtype=jnp.int32)[:, None] * (EXPERTS * CAP) + target).reshape(-1)
    picked = by_block[flat_index].reshape(BATCH, 2, D).astype(jnp.float32)
    combined = lax.optimization_barrier(jnp.sum(mixing[:, :, None] * picked, axis=1))
    return (hidden.astype(jnp.float32) + combined).astype(jnp.bfloat16)
```

```python
import math

import jax
import jax.numpy as jnp
from jax import lax
from jax.experimental import pallas as pl
from jax.experimental.pallas import tpu as pltpu
from jax.sharding import Mesh
from jax.sharding import PartitionSpec as P

norm_epsilon = 1e-05
f32 = jnp.float32
bf16 = jnp.bfloat16
last_with_last = (((1,), (1,)), ((), ()))
LOW = 16
SLOT = 32


def params(megabytes):
    return pltpu.CompilerParams(vmem_limit_bytes=megabytes << 20)


def lane_pick(values, lane):
    at = lax.broadcasted_iota(jnp.int32, values.shape, 1)
    return jnp.sum(jnp.where(at == lane, values, 0.0), axis=1, keepdims=True)


def high_part(values):
    return values.astype(bf16).astype(f32)


def attend_kernel(lengths, q_ref, k_ref, v_ref, nk_ref, nv_ref, out_ref):
    heads, tokens, head_size = q_ref.shape
    slots = k_ref.shape[1]
    rows = heads * tokens
    columns = tokens * slots
    scale = 1.0 / math.sqrt(head_size)
    queries = q_ref[...]
    scores = (
        lax.dot_general(
            queries.reshape(rows, head_size),
            k_ref[...].reshape(columns, head_size),
            last_with_last,
            preferred_element_type=f32,
        )
        * scale
    )
    column = lax.broadcasted_iota(jnp.int32, (1, columns), 1)
    owner = jnp.full((1, columns), -1, jnp.int32)
    for token in range(tokens):
        inside = (column >= token * slots) & (column < token * slots + lengths[token])
        owner = jnp.where(inside, token, owner)
    row_token = lax.broadcasted_iota(jnp.int32, (rows, 1), 0) & (tokens - 1)
    scores = jnp.where(row_token == owner, scores, -1e30)
    fresh = (
        jnp.sum(
            queries.astype(f32) * nk_ref[...].astype(f32)[None], axis=-1, keepdims=True
        ).reshape(rows, 1)
        * scale
    )
    highest = jnp.maximum(jnp.max(scores, axis=1, keepdims=True), fresh)
    weights = jnp.exp(scores - highest)
    fresh_weight = jnp.exp(fresh - highest)
    inverse = 1.0 / (jnp.sum(weights, axis=1, keepdims=True) + fresh_weight)
    probs = (weights * inverse).astype(bf16)
    fresh_prob = high_part(fresh_weight * inverse)
    fresh_values = jnp.broadcast_to(
        nv_ref[...].astype(f32)[None], (heads, tokens, head_size)
    ).reshape(rows, head_size)
    attended = jnp.dot(probs, v_ref[...].reshape(columns, head_size), preferred_element_type=f32)
    attended = (attended + fresh_prob * fresh_values).astype(bf16)
    for head in range(heads):
        block = attended[head * tokens : (head + 1) * tokens]
        for target in range(out_ref.shape[0]):
            out_ref[target, :, head * head_size : (head + 1) * head_size] = block


def project_kernel(where, own_ref, other_ref, weight_ref, residual_ref, hidden_ref, copies_ref, acc_ref):
    step = pl.program_id(0)
    sections, _, tokens, width = own_ref.shape
    core = where[0]

    @pl.when(step == 0)
    def _():
        acc_ref[...] = residual_ref[...].astype(f32)

    own_at = pl.multiple_of(core * width, 128)
    other_at = pl.multiple_of((1 - core) * width, 128)
    acc_ref[...] += lax.dot_general(
        own_ref[...].reshape(sections * tokens, width),
        weight_ref[:, pl.ds(own_at, width)],
        last_with_last,
        preferred_element_type=f32,
    ) + lax.dot_general(
        other_ref[...].reshape(sections * tokens, width),
        weight_ref[:, pl.ds(other_at, width)],
        last_with_last,
        preferred_element_type=f32,
    )

    @pl.when(step == pl.num_programs(0) - 1)
    def _():
        hidden = acc_ref[...].astype(bf16)
        hidden_ref[...] = hidden
        for target in range(copies_ref.shape[0]):
            copies_ref[target] = hidden


def dispatch_kernel(
    where, own_ref, other_ref, routes_ref, gain_ref, router_ref, out_ref, stats_ref, wide_ref
):
    pairs, tokens, width = own_ref.shape
    experts, capacity, _ = out_ref.shape
    first = where[0] == 0
    for pair in range(pairs):
        own = own_ref[pair].astype(f32)
        other = other_ref[pair].astype(f32)
        wide_ref[:, 2 * pair * width : (2 * pair + 1) * width] = jnp.where(first, own, other)
        wide_ref[:, (2 * pair + 1) * width : (2 * pair + 2) * width] = jnp.where(first, other, own)
    wide = wide_ref[...]
    squares = jnp.sum(wide * wide, axis=1, keepdims=True)
    logits = lax.dot_general(
        (wide * gain_ref[...]).astype(bf16),
        router_ref[...],
        last_with_last,
        preferred_element_type=f32,
    )
    stats_ref[...] = jnp.zeros(stats_ref.shape, f32)
    stats_ref[:, :experts] = high_part(logits)
    stats_ref[:, experts : experts + 1] = high_part(squares)
    stats_ref[:, LOW : LOW + experts] = logits - high_part(logits)
    stats_ref[:, LOW + experts : LOW + experts + 1] = squares - high_part(squares)

    routes = routes_ref[...]
    expert = lax.broadcasted_iota(jnp.int32, (experts, tokens), 0)
    named = [jnp.where(expert == routes[k : k + 1], 1.0, 0.0) for k in range(2)]
    before = jnp.where(
        lax.broadcasted_iota(jnp.int32, (tokens, tokens), 0)
        < lax.broadcasted_iota(jnp.int32, (tokens, tokens), 1),
        1.0,
        0.0,
    )
    earlier = jnp.dot(
        (named[0] + named[1]).astype(bf16), before.astype(bf16), preferred_element_type=f32
    )
    row = lax.broadcasted_iota(jnp.int32, (experts * capacity, tokens), 0)
    taken = jnp.zeros((experts * capacity, tokens), f32)
    for k in range(2):
        slot = jnp.sum(named[k] * earlier, axis=0, keepdims=True).astype(jnp.int32)
        taken = jnp.where(row == routes[k : k + 1] * capacity + slot, 1.0, taken)
    rows = jnp.dot(taken.astype(bf16), wide.astype(bf16), preferred_element_type=f32)
    out_ref[...] = rows.astype(bf16).reshape(out_ref.shape)


def expand_kernel(x_ref, gain_ref, stats_ref, gate_ref, up_ref, out_ref, scaled_ref):
    step = pl.program_id(0)
    groups, rows, total = out_ref.shape
    tile = gate_ref.shape[1]
    hidden_units = (total - 128) // 2

    @pl.when(step == 0)
    def _():
        x = x_ref[...].astype(f32).reshape(scaled_ref.shape)
        squares = jnp.sum(x * x, axis=1, keepdims=True)
        scaled_ref[...] = (x * gain_ref[...]).astype(bf16)
        high = high_part(squares)
        lane = lax.broadcasted_iota(jnp.int32, (groups * rows, 128), 1)
        stats = jnp.broadcast_to(stats_ref[...][None], (groups, rows, 128))
        extra = jnp.where(
            lane == SLOT,
            high,
            jnp.where(lane == SLOT + 1, squares - high, stats.reshape(groups * rows, 128)),
        )
        out_ref[:, :, 2 * hidden_units :] = extra.astype(bf16).reshape(groups, rows, 128)

    scaled = scaled_ref[...]
    for base, weight_ref in ((0, gate_ref), (hidden_units, up_ref)):
        product = jnp.dot(scaled, weight_ref[...], preferred_element_type=f32)
        at = pl.multiple_of(base + step * tile, 128)
        out_ref[:, :, pl.ds(at, tile)] = product.astype(bf16).reshape(groups, rows, tile)


def activate_kernel(parts_ref, routes_ref, out_ref, combine_ref, *, features, capacity):
    sections, tokens, total = parts_ref.shape
    hidden_units = (total - 128) // 2

    def summed(start, size):
        value = parts_ref[0, :, start : start + size].astype(f32)
        for section in range(1, sections):
            value = value + parts_ref[section, :, start : start + size].astype(f32)
        return value

    stats = summed(2 * hidden_units, 128)
    slot_squares = lane_pick(stats, SLOT) + lane_pick(stats, SLOT + 1)
    slot_scale = lax.rsqrt(slot_squares * (1.0 / features) + norm_epsilon)
    gate = summed(0, hidden_units) * slot_scale
    up = summed(hidden_units, hidden_units) * slot_scale
    out_ref[...] = (gate / (1.0 + jnp.exp(-gate)) * up).astype(bf16)

    experts = combine_ref.shape[1] // capacity
    lane = lax.broadcasted_iota(jnp.int32, (tokens, 128), 1)
    full = stats + pltpu.roll(stats, 128 - LOW, 1)
    token_scale = lax.rsqrt(lane_pick(full, experts) * (1.0 / features) + norm_epsilon)
    route = [routes_ref[:, k : k + 1] for k in range(2)]
    named = [jnp.where(lane == route[k], 1.0, 0.0) for k in range(2)]
    before = jnp.where(
        lax.broadcasted_iota(jnp.int32, (tokens, tokens), 1)
        < lax.broadcasted_iota(jnp.int32, (tokens, tokens), 0),
        1.0,
        0.0,
    )
    earlier = jnp.dot(
        before.astype(bf16), (named[0] + named[1]).astype(bf16), preferred_element_type=f32
    )
    chosen = [jnp.sum(named[k] * full, axis=1, keepdims=True) * token_scale for k in range(2)]
    column = lax.broadcasted_iota(jnp.int32, combine_ref.shape, 1)
    combine = jnp.zeros(combine_ref.shape, f32)
    for k in range(2):
        slot = jnp.sum(named[k] * earlier, axis=1, keepdims=True).astype(jnp.int32)
        mixing = 1.0 / (1.0 + jnp.exp(chosen[1 - k] - chosen[k]))
        combine = jnp.where(column == route[k] * capacity + slot, mixing, combine)
    combine_ref[...] = combine


def contract_kernel(where, a0_ref, a1_ref, a2_ref, a3_ref, weight_ref, out_ref, rows_ref):
    pieces = (a0_ref, a1_ref, a2_ref, a3_ref)
    rows = a0_ref.shape[0]

    @pl.when(pl.program_id(0) == 0)
    def _():
        for k, piece in enumerate(pieces):
            source = lax.rem(where[1] + len(pieces) - k, len(pieces))
            rows_ref[source] = piece[...]

    full = rows_ref[...].reshape(len(pieces) * rows, rows_ref.shape[2])
    product = jnp.dot(full, weight_ref[...], preferred_element_type=f32)
    out_ref[...] = product.astype(bf16).reshape(out_ref.shape)


def combine_kernel(where, y_ref, combine_ref, keep_ref, give_ref, wide_ref):
    pairs, tokens, width = keep_ref.shape
    first = where[0] == 0
    y = y_ref[...].reshape(combine_ref.shape[1], y_ref.shape[2])
    combine = combine_ref[...]
    high = combine.astype(bf16)
    low = (combine - high.astype(f32)).astype(bf16)
    wide_ref[...] = jnp.dot(high, y, preferred_element_type=f32) + jnp.dot(
        low, y, preferred_element_type=f32
    )
    for pair in range(pairs):
        even = wide_ref[:, 2 * pair * width : (2 * pair + 1) * width]
        odd = wide_ref[:, (2 * pair + 1) * width : (2 * pair + 2) * width]
        keep_ref[pair] = jnp.where(first, even, odd)
        give_ref[pair] = jnp.where(first, odd, even).astype(bf16)


def whole(shape):
    return pl.BlockSpec(shape, lambda *_: (0,) * len(shape))


def exchange(values, axis):
    return lax.all_to_all(values, axis, split_axis=0, concat_axis=0, tiled=True)


def swap(values):
    return lax.ppermute(values, "core", [(0, 1), (1, 0)])


def per_device(
    queries,
    key_cache,
    cached_values,
    incoming_keys,
    incoming_values,
    lengths,
    residual,
    out_proj,
    norm_gain,
    router,
    gate_proj,
    up_proj,
    down_proj,
    routes,
):
    sections = lax.axis_size("sect")
    ranks = lax.axis_size("zhi")
    section = lax.axis_index("sect")
    where = jnp.stack([lax.axis_index("core"), section]).astype(jnp.int32)
    _, tokens, heads, head_size = queries.shape
    slots = key_cache.shape[3]
    width = heads * head_size
    group, columns = residual.shape
    experts = router.shape[1]
    capacity = group // 2
    features = norm_gain.shape[0]
    share = features // sections
    hidden_units = gate_proj.shape[2]
    spread = sections * ranks
    struct = jax.ShapeDtypeStruct

    attended = pl.pallas_call(
        attend_kernel,
        grid_spec=pltpu.PrefetchScalarGridSpec(
            num_scalar_prefetch=1,
            grid=(1,),
            in_specs=[
                whole((heads, tokens, head_size)),
                whole((tokens, slots, head_size)),
                whole((tokens, slots, head_size)),
                whole((tokens, head_size)),
                whole((tokens, head_size)),
            ],
            out_specs=whole((spread, tokens, width)),
        ),
        out_shape=struct((spread, tokens, width), bf16),
        compiler_params=params(32),
        name="attend",
    )(
        lengths[0],
        jnp.swapaxes(queries[0], 0, 1),
        key_cache.reshape(tokens, slots, head_size),
        cached_values.reshape(tokens, slots, head_size),
        incoming_keys.reshape(tokens, head_size),
        incoming_values.reshape(tokens, head_size),
    )
    own = exchange(attended, ("sect", "zhi"))
    other = swap(own)
    cut = (sections, ranks, tokens, width)
    block = pl.BlockSpec((sections, 1, tokens, width), lambda i, _: (0, i, 0, 0))
    hidden, copies = pl.pallas_call(
        project_kernel,
        grid_spec=pltpu.PrefetchScalarGridSpec(
            num_scalar_prefetch=1,
            grid=(ranks,),
            in_specs=[
                block,
                block,
                pl.BlockSpec((columns, 2 * width), lambda i, _: (0, i)),
                whole((group, columns)),
            ],
            out_specs=[whole((group, columns)), whole((ranks, group, columns))],
            scratch_shapes=[pltpu.VMEM((group, columns), f32)],
        ),
        out_shape=[struct((group, columns), bf16), struct((ranks, group, columns), bf16)],
        compiler_params=params(32),
        name="project",
    )(where, own.reshape(cut), other.reshape(cut), out_proj.T, residual)

    own = exchange(copies, "zhi")
    other = swap(own)
    gain = norm_gain.reshape(1, features)
    outgoing, stats = pl.pallas_call(
        dispatch_kernel,
        grid_spec=pltpu.PrefetchScalarGridSpec(
            num_scalar_prefetch=1,
            grid=(1,),
            in_specs=[
                whole((ranks, group, columns)),
                whole((ranks, group, columns)),
                whole((2, group)),
                pl.BlockSpec((1, share), lambda i, at: (0, at[1])),
                pl.BlockSpec((experts, share), lambda i, at: (0, at[1])),
            ],
            out_specs=[whole((experts, capacity, share)), whole((group, 128))],
            scratch_shapes=[pltpu.VMEM((group, share), f32)],
        ),
        out_shape=[struct((experts, capacity, share), bf16), struct((group, 128), f32)],
        compiler_params=params(32),
        name="dispatch",
    )(where, own, other, routes.T, gain, router.T)

    arrived = exchange(outgoing, "dp")
    tile = 256
    rows = experts * capacity // sections
    total = 2 * hidden_units + 128

    def expand(at, x_ref, gain_ref, stats_ref, gate_ref, up_ref, out_ref, scaled_ref):
        expand_kernel(x_ref, gain_ref, stats_ref, gate_ref, up_ref, out_ref, scaled_ref)

    partial = pl.pallas_call(
        expand,
        grid_spec=pltpu.PrefetchScalarGridSpec(
            num_scalar_prefetch=1,
            grid=(hidden_units // tile,),
            in_specs=[
                whole((experts, capacity, share)),
                pl.BlockSpec((1, share), lambda i, at: (0, at[1])),
                whole((group, 128)),
                pl.BlockSpec((share, tile), lambda i, at: (0, i)),
                pl.BlockSpec((share, tile), lambda i, at: (0, i)),
            ],
            out_specs=whole((sections, rows, total)),
            scratch_shapes=[pltpu.VMEM((experts * capacity, share), bf16)],
        ),
        out_shape=struct((sections, rows, total), bf16),
        compiler_params=params(40),
        name="expand",
    )(where, arrived, gain, stats, gate_proj[0], up_proj[0])

    parts = exchange(partial, "sect")

    def activate(parts_ref, routes_ref, out_ref, combine_ref):
        activate_kernel(
            parts_ref, routes_ref, out_ref, combine_ref, features=features, capacity=capacity
        )

    activated, combine = pl.pallas_call(
        activate,
        out_shape=[struct((rows, hidden_units), bf16), struct((group, experts * capacity), f32)],
        compiler_params=params(32),
        name="activate",
    )(parts, routes)

    pieces = [activated] + [
        lax.ppermute(activated, "sect", [(i, (i + k) % sections) for i in range(sections)])
        for k in range(1, sections)
    ]
    down_tile = 512
    outputs = pl.pallas_call(
        contract_kernel,
        grid_spec=pltpu.PrefetchScalarGridSpec(
            num_scalar_prefetch=1,
            grid=(share // down_tile,),
            in_specs=[whole((rows, hidden_units))] * 4
            + [pl.BlockSpec((hidden_units, down_tile), lambda i, _: (0, i))],
            out_specs=pl.BlockSpec((experts, capacity, down_tile), lambda i, _: (0, 0, i)),
            scratch_shapes=[pltpu.VMEM((sections, rows, hidden_units), bf16)],
        ),
        out_shape=struct((experts, capacity, share), bf16),
        compiler_params=params(32),
        name="contract",
    )(where, *pieces, down_proj[0])

    returned = exchange(outputs, "dp")
    keep, give = pl.pallas_call(
        combine_kernel,
        grid_spec=pltpu.PrefetchScalarGridSpec(
            num_scalar_prefetch=1,
            grid=(1,),
            in_specs=[whole((experts, capacity, share)), whole((group, experts * capacity))],
            out_specs=[whole((ranks, group, columns)), whole((ranks, group, columns))],
            scratch_shapes=[pltpu.VMEM((group, share), f32)],
        ),
        out_shape=[
            struct((ranks, group, columns), f32),
            struct((ranks, group, columns), bf16),
        ],
        compiler_params=params(32),
        name="combine",
    )(where, returned, combine)
    halves = (keep + swap(give).astype(f32)).astype(bf16)
    last = exchange(halves, "zhi").astype(f32)
    return (hidden.astype(f32) + jnp.sum(last, axis=0)).astype(bf16)


def solution(mesh):
    sections, blocks, ranks = (mesh.shape[axis] for axis in ("sect", "dp", "tp"))
    devices = mesh.devices.reshape(sections, blocks, ranks // 2, 2)
    fine = Mesh(devices, ("sect", "dp", "zhi", "core"))
    tp = ("zhi", "core")
    placed = (
        P("dp", "sect", tp, None),
        P("dp", "sect", tp, None, None),
        P("dp", "sect", tp, None, None),
        P("dp", "sect", tp, None),
        P("dp", "sect", tp, None),
        P("dp", "sect"),
        P("dp", ("sect",) + tp),
        P(None, ("sect",) + tp),
        P(),
        P(),
        P("dp", "sect", tp),
        P("dp", "sect", tp),
        P("dp", tp, "sect"),
        P("dp", None),
    )
    return jax.shard_map(
        per_device, mesh=fine, in_specs=placed, out_specs=P("dp", ("sect",) + tp), check_vma=False
    )
```

```python
import math

import jax
import jax.numpy as jnp
from jax import lax
from jax.experimental import pallas as pl
from jax.experimental.pallas import tpu as pltpu
from jax.sharding import Mesh
from jax.sharding import PartitionSpec as P

norm_epsilon = 1e-05
f32 = jnp.float32
bf16 = jnp.bfloat16
last_with_last = (((1,), (1,)), ((), ()))
LOW = 16
SLOT = 32


def lane_pick(values, lane):
    at = lax.broadcasted_iota(jnp.int32, values.shape, 1)
    return jnp.sum(jnp.where(at == lane, values, 0.0), axis=1, keepdims=True)


def high_part(values):
    return values.astype(bf16).astype(f32)


def attend_kernel(
    lengths_hbm, q_hbm, k_hbm, v_hbm, nk_hbm, nv_hbm, out_ref, lengths, q_ref, k_ref, v_ref, nk_ref, nv_ref, sems
):
    copies = [
        pltpu.make_async_copy(source, target, sems.at[i])
        for i, (source, target) in enumerate(
            (
                (k_hbm, k_ref),
                (q_hbm, q_ref),
                (lengths_hbm, lengths),
                (nk_hbm, nk_ref),
                (nv_hbm, nv_ref),
                (v_hbm, v_ref),
            )
        )
    ]
    for copy in copies:
        copy.start()
    for copy in copies[:4]:
        copy.wait()
    heads, tokens, head_size = q_ref.shape
    slots = k_ref.shape[1]
    rows = heads * tokens
    columns = tokens * slots
    scale = 1.0 / math.sqrt(head_size)
    queries = q_ref[...]
    scores = (
        lax.dot_general(
            queries.reshape(rows, head_size),
            k_ref[...].reshape(columns, head_size),
            last_with_last,
            preferred_element_type=f32,
        )
        * scale
    )
    column = lax.broadcasted_iota(jnp.int32, (1, columns), 1)
    owner = jnp.full((1, columns), -1, jnp.int32)
    for token in range(tokens):
        inside = (column >= token * slots) & (column < token * slots + lengths[token])
        owner = jnp.where(inside, token, owner)
    row_token = lax.broadcasted_iota(jnp.int32, (rows, 1), 0) & (tokens - 1)
    scores = jnp.where(row_token == owner, scores, -1e30)
    fresh = (
        jnp.sum(
            queries.astype(f32) * nk_ref[...].astype(f32)[None], axis=-1, keepdims=True
        ).reshape(rows, 1)
        * scale
    )
    highest = jnp.maximum(jnp.max(scores, axis=1, keepdims=True), fresh)
    weights = jnp.exp(scores - highest)
    fresh_weight = jnp.exp(fresh - highest)
    inverse = 1.0 / (jnp.sum(weights, axis=1, keepdims=True) + fresh_weight)
    probs = (weights * inverse).astype(bf16)
    fresh_prob = high_part(fresh_weight * inverse)
    for copy in copies[4:]:
        copy.wait()
    fresh_values = jnp.broadcast_to(
        nv_ref[...].astype(f32)[None], (heads, tokens, head_size)
    ).reshape(rows, head_size)
    attended = jnp.dot(probs, v_ref[...].reshape(columns, head_size), preferred_element_type=f32)
    attended = (attended + fresh_prob * fresh_values).astype(bf16)
    for head in range(heads):
        block = attended[head * tokens : (head + 1) * tokens]
        for target in range(out_ref.shape[0]):
            out_ref[target, :, head * head_size : (head + 1) * head_size] = block


def project_kernel(*refs):
    own, other = refs[:4], refs[4:8]
    weight_ref, residual_ref, hidden_ref, copies_ref = refs[8:]
    core = lax.axis_index("core")
    section = lax.axis_index("sect")
    ranks, tokens, width = own[0].shape
    total = None
    for rank in range(ranks):
        for pieces, odd in ((own, core), (other, 1 - core)):
            rows = jnp.concatenate([piece[rank] for piece in pieces], axis=0)
            at = pl.multiple_of((2 * rank + odd) * width, 128)
            product = lax.dot_general(
                rows, weight_ref[:, pl.ds(at, width)], last_with_last, preferred_element_type=f32
            )
            total = product if total is None else total + product
    for k in range(len(own)):
        at = pl.multiple_of(lax.rem(section + len(own) - k, len(own)) * tokens, tokens)
        hidden = residual_ref[pl.ds(at, tokens), :].astype(f32) + total[k * tokens : (k + 1) * tokens]
        hidden_ref[pl.ds(at, tokens), :] = hidden.astype(bf16)
    for target in range(copies_ref.shape[0]):
        copies_ref[target] = hidden_ref[...]


def dispatch_kernel(half_ref, routes_ref, gain_ref, router_ref, out_ref, stats_ref, wide_ref, side_ref):
    pairs, tokens, width = half_ref.shape
    experts, capacity, half = out_ref.shape
    share = 2 * half
    first = lax.axis_index("core") == 0
    at = pl.multiple_of(lax.axis_index("sect") * share, 128)
    gain = gain_ref[:, pl.ds(at, share)]
    router = router_ref[:, pl.ds(at, share)].astype(f32)
    for pair in range(pairs):
        here = slice(pair * width, (pair + 1) * width)
        even = slice(2 * pair * width, (2 * pair + 1) * width)
        odd = slice((2 * pair + 1) * width, (2 * pair + 2) * width)
        wide_ref[:, here] = half_ref[pair].astype(f32)
        side_ref[0:experts, here] = jnp.where(first, router[:, even], router[:, odd])
        side_ref[experts : experts + 1, here] = jnp.where(first, gain[:, even], gain[:, odd])
    wide = wide_ref[...]
    squares = jnp.sum(wide * wide, axis=1, keepdims=True)
    logits = lax.dot_general(
        (wide * side_ref[experts : experts + 1, :]).astype(bf16),
        side_ref[0:experts, :].astype(bf16),
        last_with_last,
        preferred_element_type=f32,
    )
    stats_ref[...] = jnp.zeros(stats_ref.shape, f32)
    stats_ref[:, :experts] = logits
    stats_ref[:, experts : experts + 1] = squares

    routes = routes_ref[...]
    expert = lax.broadcasted_iota(jnp.int32, (experts, tokens), 0)
    named = [jnp.where(expert == routes[k : k + 1], 1.0, 0.0) for k in range(2)]
    before = jnp.where(
        lax.broadcasted_iota(jnp.int32, (tokens, tokens), 0)
        < lax.broadcasted_iota(jnp.int32, (tokens, tokens), 1),
        1.0,
        0.0,
    )
    earlier = jnp.dot(
        (named[0] + named[1]).astype(bf16), before.astype(bf16), preferred_element_type=f32
    )
    row = lax.broadcasted_iota(jnp.int32, (experts * capacity, tokens), 0)
    taken = jnp.zeros((experts * capacity, tokens), f32)
    for k in range(2):
        slot = jnp.sum(named[k] * earlier, axis=0, keepdims=True).astype(jnp.int32)
        taken = jnp.where(row == routes[k : k + 1] * capacity + slot, 1.0, taken)
    rows = jnp.dot(taken.astype(bf16), wide.astype(bf16), preferred_element_type=f32)
    out_ref[...] = rows.astype(bf16).reshape(out_ref.shape)


def expand_kernel(
    own_ref, other_ref, own_stats, other_stats, gain_ref, gate_ref, up_ref, *rest
):
    outs, wide_ref, scaled_ref = rest[:4], rest[4], rest[5]
    sections = len(outs)
    rows, total = outs[0].shape
    blocks, capacity, half = own_ref.shape
    share = 2 * half
    hidden_units = (total - 128) // 2
    pairs = 4
    width = half // pairs
    first = lax.axis_index("core") == 0
    section = lax.axis_index("sect")
    per = blocks // sections
    for k in range(sections):
        at = lax.rem(section + k, sections) * per
        own = own_ref[pl.ds(at, per)].astype(f32).reshape(rows, half)
        other = other_ref[pl.ds(at, per)].astype(f32).reshape(rows, half)
        for pair in range(pairs):
            mine = own[:, pair * width : (pair + 1) * width]
            theirs = other[:, pair * width : (pair + 1) * width]
            even = 2 * pair * width
            odd = even + width
            wide_ref[k * rows : (k + 1) * rows, even:odd] = jnp.where(first, mine, theirs)
            wide_ref[k * rows : (k + 1) * rows, odd : odd + width] = jnp.where(first, theirs, mine)
    gain = gain_ref[:, pl.ds(pl.multiple_of(section * share, 128), share)]
    stats = own_stats[...] + other_stats[...]
    high = high_part(stats)
    stats = high + pltpu.roll(stats - high, LOW, 1)
    lane = lax.broadcasted_iota(jnp.int32, (rows, 128), 1)
    for k in range(sections):
        x = wide_ref[k * rows : (k + 1) * rows, :]
        squares = jnp.sum(x * x, axis=1, keepdims=True)
        scaled_ref[k * rows : (k + 1) * rows, :] = (x * gain).astype(bf16)
        high = high_part(squares)
        extra = jnp.where(lane == SLOT, high, jnp.where(lane == SLOT + 1, squares - high, stats))
        outs[k][:, 2 * hidden_units :] = extra.astype(bf16)

    tile = 256

    def step(i, carry):
        for base, weight_ref in ((0, gate_ref), (hidden_units, up_ref)):
            source = pl.multiple_of(i * tile, tile)
            product = jnp.dot(
                scaled_ref[...], weight_ref[:, pl.ds(source, tile)], preferred_element_type=f32
            ).astype(bf16)
            target = pl.multiple_of(base + i * tile, tile)
            for k in range(sections):
                outs[k][:, pl.ds(target, tile)] = product[k * rows : (k + 1) * rows]
        return carry

    lax.fori_loop(0, hidden_units // tile, step, 0)


def activate_kernel(
    part0, part1, part2, part3, routes_ref, out_ref, combine_ref, *, features, capacity
):
    parts = (part0, part1, part2, part3)
    tokens, total = part0.shape
    hidden_units = (total - 128) // 2

    def summed(start, size):
        value = parts[0][:, start : start + size].astype(f32)
        for part in parts[1:]:
            value = value + part[:, start : start + size].astype(f32)
        return value

    stats = summed(2 * hidden_units, 128)
    slot_squares = lane_pick(stats, SLOT) + lane_pick(stats, SLOT + 1)
    slot_scale = lax.rsqrt(slot_squares * (1.0 / features) + norm_epsilon)
    gate = summed(0, hidden_units) * slot_scale
    up = summed(hidden_units, hidden_units) * slot_scale
    out_ref[...] = (gate / (1.0 + jnp.exp(-gate)) * up).astype(bf16)

    experts = combine_ref.shape[1] // capacity
    lane = lax.broadcasted_iota(jnp.int32, (tokens, 128), 1)
    full = stats + pltpu.roll(stats, 128 - LOW, 1)
    token_scale = lax.rsqrt(lane_pick(full, experts) * (1.0 / features) + norm_epsilon)
    at_row = lax.broadcasted_iota(jnp.int32, (tokens, tokens), 0)
    at_lane = lax.broadcasted_iota(jnp.int32, (tokens, tokens), 1)
    before = jnp.where(at_lane < at_row, 1.0, 0.0)
    route = [
        jnp.sum(
            jnp.where(at_row == at_lane, routes_ref[k : k + 1, :].astype(f32), 0.0),
            axis=1,
            keepdims=True,
        ).astype(jnp.int32)
        for k in range(2)
    ]
    named = [jnp.where(lane == route[k], 1.0, 0.0) for k in range(2)]
    earlier = jnp.dot(
        before.astype(bf16), (named[0] + named[1]).astype(bf16), preferred_element_type=f32
    )
    chosen = [jnp.sum(named[k] * full, axis=1, keepdims=True) * token_scale for k in range(2)]
    column = lax.broadcasted_iota(jnp.int32, combine_ref.shape, 1)
    combine = jnp.zeros(combine_ref.shape, f32)
    for k in range(2):
        slot = jnp.sum(named[k] * earlier, axis=1, keepdims=True).astype(jnp.int32)
        mixing = 1.0 / (1.0 + jnp.exp(chosen[1 - k] - chosen[k]))
        combine = jnp.where(column == route[k] * capacity + slot, mixing, combine)
    combine_ref[...] = combine


def contract_kernel(a0_ref, a1_ref, a2_ref, a3_ref, weight_ref, keep_ref, give_ref, rows_ref, give_wide):
    pieces = (a0_ref, a1_ref, a2_ref, a3_ref)
    rows = a0_ref.shape[0]
    blocks, capacity, half = keep_ref.shape
    pairs = 4
    width = half // pairs
    first = lax.axis_index("core") == 0
    section = lax.axis_index("sect")
    for k, piece in enumerate(pieces):
        rows_ref[lax.rem(section + len(pieces) - k, len(pieces))] = piece[...]
    full = rows_ref[...].reshape(len(pieces) * rows, rows_ref.shape[2])
    for chunk in range(2):
        product = jnp.dot(
            full, weight_ref[:, chunk * half : (chunk + 1) * half], preferred_element_type=f32
        )
        for pair in range(pairs // 2):
            even = product[:, 2 * pair * width : (2 * pair + 1) * width]
            odd = product[:, (2 * pair + 1) * width : (2 * pair + 2) * width]
            at = (chunk * (pairs // 2) + pair) * width
            kept = jnp.where(first, even, odd)
            keep_ref[:, :, at : at + width] = kept.reshape(blocks, capacity, width)
            give_wide[:, at : at + width] = jnp.where(first, odd, even)
    give_ref[...] = give_wide[...].astype(bf16).reshape(give_ref.shape)


def combine_kernel(y_ref, combine_ref, out_ref, wide_ref):
    pairs, tokens, width = out_ref.shape
    y = y_ref[...].reshape(combine_ref.shape[1], y_ref.shape[2])
    combine = combine_ref[...]
    high = combine.astype(bf16)
    low = (combine - high.astype(f32)).astype(bf16)
    wide_ref[...] = jnp.dot(high, y, preferred_element_type=f32) + jnp.dot(
        low, y, preferred_element_type=f32
    )
    for pair in range(pairs):
        out_ref[pair] = wide_ref[:, pair * width : (pair + 1) * width].astype(bf16)


def exchange(values, axis):
    return lax.all_to_all(values, axis, split_axis=0, concat_axis=0, tiled=True)


def swap(values):
    return lax.ppermute(values, "core", [(0, 1), (1, 0)])


def around(pieces):
    sections = len(pieces)
    arrived = list(pieces)
    for k in (2, 1, 3):
        arrived[k] = lax.ppermute(
            pieces[k], "sect", [(i, (i + k) % sections) for i in range(sections)]
        )
    return arrived


def call(kernel, name, out_shape, in_specs=None, scratch_shapes=()):
    extra = {} if in_specs is None else {"in_specs": in_specs}
    return pl.pallas_call(
        kernel,
        out_shape=out_shape,
        scratch_shapes=scratch_shapes,
        compiler_params=pltpu.CompilerParams(vmem_limit_bytes=16 << 20),
        name=name,
        **extra,
    )


def per_device(
    queries,
    key_cache,
    cached_values,
    incoming_keys,
    incoming_values,
    lengths,
    residual,
    out_proj,
    norm_gain,
    router,
    gate_proj,
    up_proj,
    down_proj,
    routes,
):
    sections = lax.axis_size("sect")
    ranks = lax.axis_size("zhi")
    _, tokens, heads, head_size = queries.shape
    slots = key_cache.shape[3]
    width = heads * head_size
    group, columns = residual.shape
    experts = router.shape[1]
    capacity = group // 2
    features = norm_gain.shape[0]
    half = features // sections // 2
    hidden_units = gate_proj.shape[2]
    rows = experts * capacity // sections
    struct = jax.ShapeDtypeStruct
    vmem = pltpu.VMEM

    attended = call(
        attend_kernel,
        "attend",
        struct((ranks, tokens, width), bf16),
        [pl.BlockSpec(memory_space=pltpu.HBM)] * 6,
        [
            pltpu.SMEM((tokens,), jnp.int32),
            vmem((heads, tokens, head_size), bf16),
            vmem((tokens, slots, head_size), bf16),
            vmem((tokens, slots, head_size), bf16),
            vmem((tokens, head_size), bf16),
            vmem((tokens, head_size), bf16),
            pltpu.SemaphoreType.DMA((6,)),
        ],
    )(
        lengths[0],
        jnp.swapaxes(queries[0], 0, 1),
        key_cache.reshape(tokens, slots, head_size),
        cached_values.reshape(tokens, slots, head_size),
        incoming_keys.reshape(tokens, head_size),
        incoming_values.reshape(tokens, head_size),
    )
    own = around([exchange(attended, "zhi")] * sections)
    other = [swap(piece) for piece in own]
    hidden, copies = call(
        project_kernel,
        "project",
        [struct((group, columns), bf16), struct((ranks, group, columns), bf16)],
    )(*own, *other, out_proj.T, residual)

    gain = norm_gain.reshape(1, features)
    outgoing, stats = call(
        dispatch_kernel,
        "dispatch",
        [struct((experts, capacity, half), bf16), struct((group, 128), f32)],
        None,
        [vmem((group, half), f32), vmem((2 * experts, half), f32)],
    )(exchange(copies, "zhi"), routes.T, gain, router.T)
    other_stats = swap(stats)
    arrived = exchange(outgoing, "dp")

    partial = call(
        expand_kernel,
        "expand",
        [struct((rows, 2 * hidden_units + 128), bf16)] * sections,
        None,
        [vmem((experts * capacity, 2 * half), f32), vmem((experts * capacity, 2 * half), bf16)],
    )(arrived, swap(arrived), stats, other_stats, gain, gate_proj[0], up_proj[0])

    def activate(*refs):
        activate_kernel(*refs, features=features, capacity=capacity)

    activated, combine = call(
        activate,
        "activate",
        [struct((rows, hidden_units), bf16), struct((group, experts * capacity), f32)],
    )(*around(partial), routes.T)

    keep, give = call(
        contract_kernel,
        "contract",
        [struct((experts, capacity, half), f32), struct((experts, capacity, half), bf16)],
        None,
        [vmem((sections, rows, hidden_units), bf16), vmem((experts * capacity, half), f32)],
    )(*around([activated] * sections), down_proj[0])
    outputs = (keep + swap(give).astype(f32)).astype(bf16)

    mixed = call(
        combine_kernel,
        "combine",
        struct((ranks, group, columns), bf16),
        None,
        [vmem((group, half), f32)],
    )(exchange(outputs, "dp"), combine)
    last = exchange(mixed, "zhi").astype(f32)
    return (hidden.astype(f32) + jnp.sum(last, axis=0)).astype(bf16)


def solution(mesh):
    sections, blocks, ranks = (mesh.shape[axis] for axis in ("sect", "dp", "tp"))
    devices = mesh.devices.reshape(sections, blocks, ranks // 2, 2)
    fine = Mesh(devices, ("sect", "dp", "zhi", "core"))
    tp = ("zhi", "core")
    placed = (
        P("dp", "sect", tp, None),
        P("dp", "sect", tp, None, None),
        P("dp", "sect", tp, None, None),
        P("dp", "sect", tp, None),
        P("dp", "sect", tp, None),
        P("dp", "sect"),
        P("dp", ("sect",) + tp),
        P(None, ("sect",) + tp),
        P(),
        P(),
        P("dp", "sect", tp),
        P("dp", "sect", tp),
        P("dp", tp, "sect"),
        P("dp", None),
    )
    return jax.shard_map(
        per_device, mesh=fine, in_specs=placed, out_specs=P("dp", ("sect",) + tp), check_vma=False
    )
```

```python
import math

import jax
import jax.numpy as jnp
from jax import lax
from jax.experimental import pallas as pl
from jax.experimental.pallas import tpu as pltpu
from jax.sharding import Mesh
from jax.sharding import PartitionSpec as P

norm_epsilon = 1e-05
f32 = jnp.float32
bf16 = jnp.bfloat16
last_with_last = (((1,), (1,)), ((), ()))
LOW = 16
SLOT = 32
FAR = 64


def lane_pick(values, lane):
    at = lax.broadcasted_iota(jnp.int32, values.shape, 1)
    return jnp.sum(jnp.where(at == lane, values, 0.0), axis=1, keepdims=True)


def high_part(values):
    return values.astype(bf16).astype(f32)


def place(routes_ref, gain_ref, router_ref, side_ref, taken_ref):
    experts = router_ref.shape[0]
    half = side_ref.shape[1]
    width = half // 4
    share = 2 * half
    slots, tokens = taken_ref.shape
    capacity = slots // experts
    first = lax.axis_index("core") == 0
    at = pl.multiple_of(lax.axis_index("sect") * share, 128)
    gain = gain_ref[:, pl.ds(at, share)]
    router = router_ref[:, pl.ds(at, share)].astype(f32)
    for pair in range(4):
        here = slice(pair * width, (pair + 1) * width)
        even = slice(2 * pair * width, (2 * pair + 1) * width)
        odd = slice((2 * pair + 1) * width, (2 * pair + 2) * width)
        side_ref[0:experts, here] = jnp.where(first, router[:, even], router[:, odd])
        side_ref[experts : experts + 1, here] = jnp.where(first, gain[:, even], gain[:, odd])
    routes = routes_ref[...]
    expert = lax.broadcasted_iota(jnp.int32, (experts, tokens), 0)
    named = [jnp.where(expert == routes[k : k + 1], 1.0, 0.0) for k in range(2)]
    before = jnp.where(
        lax.broadcasted_iota(jnp.int32, (tokens, tokens), 0)
        < lax.broadcasted_iota(jnp.int32, (tokens, tokens), 1),
        1.0,
        0.0,
    )
    earlier = jnp.dot(
        (named[0] + named[1]).astype(bf16), before.astype(bf16), preferred_element_type=f32
    )
    row = lax.broadcasted_iota(jnp.int32, (slots, tokens), 0)
    taken = jnp.zeros((slots, tokens), f32)
    for k in range(2):
        slot = jnp.sum(named[k] * earlier, axis=0, keepdims=True).astype(jnp.int32)
        taken = jnp.where(row == routes[k : k + 1] * capacity + slot, 1.0, taken)
    taken_ref[...] = taken.astype(bf16)


def attend_kernel(*refs):
    sources, outs, scratch = refs[:11], refs[11:16], refs[16:]
    out_ref, weight_ref, residual_ref, side_ref, taken_ref = outs
    lengths, q_ref, k_ref, v_ref, nk_ref, nv_ref, routes_ref, gain_ref, router_ref, sems = scratch
    targets = (
        k_ref,
        q_ref,
        lengths,
        nk_ref,
        routes_ref,
        gain_ref,
        router_ref,
        v_ref,
        nv_ref,
        weight_ref,
        residual_ref,
    )
    copies = [
        pltpu.make_async_copy(source, target, sems.at[i])
        for i, (source, target) in enumerate(zip(sources, targets, strict=True))
    ]
    for copy in copies:
        copy.start()
    for copy in copies[4:7]:
        copy.wait()
    place(routes_ref, gain_ref, router_ref, side_ref, taken_ref)
    for copy in copies[:4]:
        copy.wait()
    heads, tokens, head_size = q_ref.shape
    slots = k_ref.shape[1]
    rows = heads * tokens
    columns = tokens * slots
    scale = 1.0 / math.sqrt(head_size)
    queries = q_ref[...]
    scores = (
        lax.dot_general(
            queries.reshape(rows, head_size),
            k_ref[...].reshape(columns, head_size),
            last_with_last,
            preferred_element_type=f32,
        )
        * scale
    )
    column = lax.broadcasted_iota(jnp.int32, (1, columns), 1)
    owner = jnp.full((1, columns), -1, jnp.int32)
    for token in range(tokens):
        inside = (column >= token * slots) & (column < token * slots + lengths[token])
        owner = jnp.where(inside, token, owner)
    row_token = lax.broadcasted_iota(jnp.int32, (rows, 1), 0) & (tokens - 1)
    scores = jnp.where(row_token == owner, scores, -1e30)
    fresh = (
        jnp.sum(
            queries.astype(f32) * nk_ref[...].astype(f32)[None], axis=-1, keepdims=True
        ).reshape(rows, 1)
        * scale
    )
    highest = jnp.maximum(jnp.max(scores, axis=1, keepdims=True), fresh)
    weights = jnp.exp(scores - highest)
    fresh_weight = jnp.exp(fresh - highest)
    inverse = 1.0 / (jnp.sum(weights, axis=1, keepdims=True) + fresh_weight)
    probs = (weights * inverse).astype(bf16)
    fresh_prob = high_part(fresh_weight * inverse)
    for copy in copies[7:9]:
        copy.wait()
    fresh_values = jnp.broadcast_to(
        nv_ref[...].astype(f32)[None], (heads, tokens, head_size)
    ).reshape(rows, head_size)
    attended = jnp.dot(probs, v_ref[...].reshape(columns, head_size), preferred_element_type=f32)
    attended = (attended + fresh_prob * fresh_values).astype(bf16)
    for head in range(heads):
        block = attended[head * tokens : (head + 1) * tokens]
        for target in range(out_ref.shape[0]):
            out_ref[target, :, head * head_size : (head + 1) * head_size] = block
    for copy in copies[9:]:
        copy.wait()


def project_kernel(*refs):
    own, other = refs[:4], refs[4:8]
    weight_ref, residual_ref, hidden_ref, copies_ref = refs[8:]
    core = lax.axis_index("core")
    section = lax.axis_index("sect")
    ranks, tokens, width = own[0].shape
    total = None
    for rank in range(ranks):
        for pieces, odd in ((own, core), (other, 1 - core)):
            rows = jnp.concatenate([piece[rank] for piece in pieces], axis=0)
            at = pl.multiple_of((2 * rank + odd) * width, 128)
            product = lax.dot_general(
                rows, weight_ref[:, pl.ds(at, width)], last_with_last, preferred_element_type=f32
            )
            total = product if total is None else total + product
    for k in range(len(own)):
        at = pl.multiple_of(lax.rem(section + len(own) - k, len(own)) * tokens, tokens)
        hidden = residual_ref[pl.ds(at, tokens), :].astype(f32) + total[k * tokens : (k + 1) * tokens]
        hidden_ref[pl.ds(at, tokens), :] = hidden.astype(bf16)
    for target in range(copies_ref.shape[0]):
        copies_ref[target] = hidden_ref[...]


def dispatch_kernel(half_ref, side_ref, taken_ref, out_ref, stats_ref, wide_ref):
    pairs, tokens, width = half_ref.shape
    experts = out_ref.shape[0]
    for pair in range(pairs):
        wide_ref[:, pair * width : (pair + 1) * width] = half_ref[pair].astype(f32)
    wide = wide_ref[...]
    squares = jnp.sum(wide * wide, axis=1, keepdims=True)
    logits = lax.dot_general(
        (wide * side_ref[experts : experts + 1, :]).astype(bf16),
        side_ref[0:experts, :].astype(bf16),
        last_with_last,
        preferred_element_type=f32,
    )
    stats_ref[...] = jnp.zeros(stats_ref.shape, f32)
    stats_ref[:, :experts] = logits
    stats_ref[:, experts : experts + 1] = squares
    rows = jnp.dot(taken_ref[...], wide.astype(bf16), preferred_element_type=f32)
    out_ref[...] = rows.astype(bf16).reshape(out_ref.shape)


def expand_kernel(
    own_ref, other_ref, own_stats, other_stats, gain_ref, gate_ref, up_ref, *rest, offsets
):
    outs, wide_ref, scaled_ref = rest[:-2], rest[-2], rest[-1]
    sections = 4
    blocks, capacity, half = own_ref.shape
    per = blocks // sections
    rows = per * capacity
    share = 2 * half
    hidden_units = gate_ref.shape[1]
    pairs = 4
    width = half // pairs
    first = lax.axis_index("core") == 0
    section = lax.axis_index("sect")
    for k, offset in enumerate(offsets):
        at = lax.rem(section + offset, sections) * per
        own = own_ref[pl.ds(at, per)].astype(f32).reshape(rows, half)
        other = other_ref[pl.ds(at, per)].astype(f32).reshape(rows, half)
        for pair in range(pairs):
            mine = own[:, pair * width : (pair + 1) * width]
            theirs = other[:, pair * width : (pair + 1) * width]
            even = 2 * pair * width
            odd = even + width
            wide_ref[k * rows : (k + 1) * rows, even:odd] = jnp.where(first, mine, theirs)
            wide_ref[k * rows : (k + 1) * rows, odd : odd + width] = jnp.where(first, theirs, mine)
    gain = gain_ref[:, pl.ds(pl.multiple_of(section * share, 128), share)]
    stats = own_stats[...] + other_stats[...]
    high = high_part(stats)
    stats = high + pltpu.roll(stats - high, LOW, 1)
    lane = lax.broadcasted_iota(jnp.int32, (rows, 128), 1)
    for k in range(len(offsets)):
        x = wide_ref[k * rows : (k + 1) * rows, :]
        squares = jnp.sum(x * x, axis=1, keepdims=True)
        scaled_ref[k * rows : (k + 1) * rows, :] = (x * gain).astype(bf16)
        high = high_part(squares)
        extra = jnp.where(lane == SLOT, high, jnp.where(lane == SLOT + 1, squares - high, stats))
        outs[2 * k][:, hidden_units:] = extra.astype(bf16)

    tile = 256

    def step(i, carry):
        at = pl.multiple_of(i * tile, tile)
        for which, weight_ref in enumerate((gate_ref, up_ref)):
            product = jnp.dot(
                scaled_ref[...], weight_ref[:, pl.ds(at, tile)], preferred_element_type=f32
            ).astype(bf16)
            for k in range(len(offsets)):
                outs[2 * k + which][:, pl.ds(at, tile)] = product[k * rows : (k + 1) * rows]
        return carry

    lax.fori_loop(0, hidden_units // tile, step, 0)


def relay_kernel(gate_ref, up_ref, far_gate_ref, far_up_ref, right_ref, left_ref, *, units):
    right_gate, left_gate = gate_ref
    right_up, left_up = up_ref
    lane = lax.broadcasted_iota(jnp.int32, (right_gate.shape[0], 128), 1)
    right_ref[:, :units] = (
        right_gate[:, :units].astype(f32) + far_gate_ref[:, :units].astype(f32)
    ).astype(bf16)
    extra = jnp.where(
        lane < FAR,
        right_gate[:, units:].astype(f32),
        pltpu.roll(far_gate_ref[:, units:].astype(f32), FAR, 1),
    )
    right_ref[:, units : units + 128] = extra.astype(bf16)
    right_ref[:, units + 128 :] = right_up[...]
    left_ref[:, : units + 128] = left_gate[...]
    left_ref[:, units + 128 :] = (left_up[...].astype(f32) + far_up_ref[...].astype(f32)).astype(bf16)


def activate_kernel(
    gate_ref, up_ref, left_ref, right_ref, routes_ref, out_ref, combine_ref, *, features, capacity
):
    tokens, hidden_units = up_ref.shape
    base = hidden_units + 128

    def summed(own, start, size):
        value = own.astype(f32)
        for part in (left_ref, right_ref):
            value = value + part[:, start : start + size].astype(f32)
        return value

    stats = summed(gate_ref[:, hidden_units:], hidden_units, 128)
    stats = stats + pltpu.roll(stats, 128 - FAR, 1)
    slot_squares = lane_pick(stats, SLOT) + lane_pick(stats, SLOT + 1)
    slot_scale = lax.rsqrt(slot_squares * (1.0 / features) + norm_epsilon)
    gate = summed(gate_ref[:, :hidden_units], 0, hidden_units) * slot_scale
    up = summed(up_ref[...], base, hidden_units) * slot_scale
    out_ref[...] = (gate / (1.0 + jnp.exp(-gate)) * up).astype(bf16)

    experts = combine_ref.shape[1] // capacity
    lane = lax.broadcasted_iota(jnp.int32, (tokens, 128), 1)
    full = stats + pltpu.roll(stats, 128 - LOW, 1)
    token_scale = lax.rsqrt(lane_pick(full, experts) * (1.0 / features) + norm_epsilon)
    at_row = lax.broadcasted_iota(jnp.int32, (tokens, tokens), 0)
    at_lane = lax.broadcasted_iota(jnp.int32, (tokens, tokens), 1)
    before = jnp.where(at_lane < at_row, 1.0, 0.0)
    route = [
        jnp.sum(
            jnp.where(at_row == at_lane, routes_ref[k : k + 1, :].astype(f32), 0.0),
            axis=1,
            keepdims=True,
        ).astype(jnp.int32)
        for k in range(2)
    ]
    named = [jnp.where(lane == route[k], 1.0, 0.0) for k in range(2)]
    earlier = jnp.dot(
        before.astype(bf16), (named[0] + named[1]).astype(bf16), preferred_element_type=f32
    )
    chosen = [jnp.sum(named[k] * full, axis=1, keepdims=True) * token_scale for k in range(2)]
    column = lax.broadcasted_iota(jnp.int32, combine_ref.shape, 1)
    combine = jnp.zeros(combine_ref.shape, f32)
    for k in range(2):
        slot = jnp.sum(named[k] * earlier, axis=1, keepdims=True).astype(jnp.int32)
        mixing = 1.0 / (1.0 + jnp.exp(chosen[1 - k] - chosen[k]))
        combine = jnp.where(column == route[k] * capacity + slot, mixing, combine)
    combine_ref[...] = combine


def contract_kernel(a0_ref, a1_ref, a2_ref, a3_ref, weight_ref, keep_ref, give_ref, rows_ref, give_wide):
    pieces = (a0_ref, a1_ref, a2_ref, a3_ref)
    rows = a0_ref.shape[0]
    blocks, capacity, half = keep_ref.shape
    pairs = 4
    width = half // pairs
    first = lax.axis_index("core") == 0
    section = lax.axis_index("sect")
    for k, piece in enumerate(pieces):
        rows_ref[lax.rem(section + len(pieces) - k, len(pieces))] = piece[...]
    full = rows_ref[...].reshape(len(pieces) * rows, rows_ref.shape[2])
    for chunk in range(2):
        product = jnp.dot(
            full, weight_ref[:, chunk * half : (chunk + 1) * half], preferred_element_type=f32
        )
        for pair in range(pairs // 2):
            even = product[:, 2 * pair * width : (2 * pair + 1) * width]
            odd = product[:, (2 * pair + 1) * width : (2 * pair + 2) * width]
            at = (chunk * (pairs // 2) + pair) * width
            kept = jnp.where(first, even, odd)
            keep_ref[:, :, at : at + width] = kept.reshape(blocks, capacity, width)
            give_wide[:, at : at + width] = jnp.where(first, odd, even)
    give_ref[...] = give_wide[...].astype(bf16).reshape(give_ref.shape)


def combine_kernel(y_ref, combine_ref, out_ref, wide_ref):
    pairs, tokens, width = out_ref.shape
    y = y_ref[...].reshape(combine_ref.shape[1], y_ref.shape[2])
    combine = combine_ref[...]
    high = combine.astype(bf16)
    low = (combine - high.astype(f32)).astype(bf16)
    wide_ref[...] = jnp.dot(high, y, preferred_element_type=f32) + jnp.dot(
        low, y, preferred_element_type=f32
    )
    for pair in range(pairs):
        out_ref[pair] = wide_ref[:, pair * width : (pair + 1) * width].astype(bf16)


def exchange(values, axis):
    return lax.all_to_all(values, axis, split_axis=0, concat_axis=0, tiled=True)


def swap(values):
    return lax.ppermute(values, "core", [(0, 1), (1, 0)])


def around(pieces):
    sections = len(pieces)
    arrived = list(pieces)
    for k in (2, 1, 3):
        arrived[k] = lax.ppermute(
            pieces[k], "sect", [(i, (i + k) % sections) for i in range(sections)]
        )
    return arrived


def call(kernel, name, out_shape, in_specs=None, scratch_shapes=()):
    extra = {} if in_specs is None else {"in_specs": in_specs}
    return pl.pallas_call(
        kernel,
        out_shape=out_shape,
        scratch_shapes=scratch_shapes,
        compiler_params=pltpu.CompilerParams(vmem_limit_bytes=16 << 20),
        name=name,
        **extra,
    )


def per_device(
    queries,
    key_cache,
    cached_values,
    incoming_keys,
    incoming_values,
    lengths,
    residual,
    out_proj,
    norm_gain,
    router,
    gate_proj,
    up_proj,
    down_proj,
    routes,
):
    sections = lax.axis_size("sect")
    ranks = lax.axis_size("zhi")
    _, tokens, heads, head_size = queries.shape
    slots = key_cache.shape[3]
    width = heads * head_size
    group, columns = residual.shape
    experts = router.shape[1]
    capacity = group // 2
    features = norm_gain.shape[0]
    half = features // sections // 2
    hidden_units = gate_proj.shape[2]
    rows = experts * capacity // sections
    struct = jax.ShapeDtypeStruct
    vmem = pltpu.VMEM

    gain = norm_gain.reshape(1, features)
    operands = (
        key_cache.reshape(tokens, slots, head_size),
        jnp.swapaxes(queries[0], 0, 1),
        lengths[0],
        incoming_keys.reshape(tokens, head_size),
        routes.T,
        gain,
        router.T,
        cached_values.reshape(tokens, slots, head_size),
        incoming_values.reshape(tokens, head_size),
        out_proj.T,
        residual,
    )
    attended, weight, residual, side, taken = call(
        attend_kernel,
        "attend",
        [
            struct((ranks, tokens, width), bf16),
            struct((columns, features), bf16),
            struct((group, columns), bf16),
            struct((2 * experts, half), f32),
            struct((experts * capacity, group), bf16),
        ],
        [pl.BlockSpec(memory_space=pltpu.HBM)] * len(operands),
        [
            pltpu.SMEM((tokens,), jnp.int32),
            vmem((heads, tokens, head_size), bf16),
            vmem((tokens, slots, head_size), bf16),
            vmem((tokens, slots, head_size), bf16),
            vmem((tokens, head_size), bf16),
            vmem((tokens, head_size), bf16),
            vmem((2, group), jnp.int32),
            vmem((1, features), f32),
            vmem((experts, features), bf16),
            pltpu.SemaphoreType.DMA((len(operands),)),
        ],
    )(*(pltpu.with_memory_space_constraint(operand, pltpu.HBM) for operand in operands))
    own = around([exchange(attended, "zhi")] * sections)
    other = [swap(piece) for piece in own]
    hidden, copies = call(
        project_kernel,
        "project",
        [struct((group, columns), bf16), struct((ranks, group, columns), bf16)],
    )(*own, *other, weight, residual)

    outgoing, stats = call(
        dispatch_kernel,
        "dispatch",
        [struct((experts, capacity, half), bf16), struct((group, 128), f32)],
        None,
        [vmem((group, half), f32)],
    )(exchange(copies, "zhi"), side, taken)
    other_stats = swap(stats)
    arrived = exchange(outgoing, "dp")
    expand_operands = (arrived, swap(arrived), stats, other_stats, gain, gate_proj[0], up_proj[0])

    def expand(name, offsets):
        def kernel(*refs):
            expand_kernel(*refs, offsets=offsets)

        count = len(offsets) * rows
        return call(
            kernel,
            name,
            [struct((rows, hidden_units + 128), bf16), struct((rows, hidden_units), bf16)]
            * len(offsets),
            None,
            [vmem((count, 2 * half), f32), vmem((count, 2 * half), bf16)],
        )(*expand_operands)

    def shift(values, by):
        pairs = [(i, (i + by) % sections) for i in range(sections)]
        return lax.ppermute(values, "sect", pairs)

    far_gate, far_up = expand("expand_far", (2,))
    far_gate, far_up = shift(far_gate, 1), shift(far_up, -1)
    own_gate, own_up, right_gate, right_up, left_gate, left_up = expand("expand_near", (0, 1, 3))

    def relay(right_gate, left_gate, right_up, left_up, *rest):
        relay_kernel((right_gate, left_gate), (right_up, left_up), *rest, units=hidden_units)

    to_right, to_left = call(
        relay, "relay", [struct((rows, 2 * hidden_units + 128), bf16)] * 2
    )(right_gate, left_gate, right_up, left_up, far_gate, far_up)

    def activate(*refs):
        activate_kernel(*refs, features=features, capacity=capacity)

    activated, combine = call(
        activate,
        "activate",
        [struct((rows, hidden_units), bf16), struct((group, experts * capacity), f32)],
    )(own_gate, own_up, shift(to_right, 1), shift(to_left, -1), routes.T)

    keep, give = call(
        contract_kernel,
        "contract",
        [struct((experts, capacity, half), f32), struct((experts, capacity, half), bf16)],
        None,
        [vmem((sections, rows, hidden_units), bf16), vmem((experts * capacity, half), f32)],
    )(*around([activated] * sections), down_proj[0])
    outputs = (keep + swap(give).astype(f32)).astype(bf16)

    mixed = call(
        combine_kernel,
        "combine",
        struct((ranks, group, columns), bf16),
        None,
        [vmem((group, half), f32)],
    )(exchange(outputs, "dp"), combine)
    last = exchange(mixed, "zhi").astype(f32)
    return (hidden.astype(f32) + jnp.sum(last, axis=0)).astype(bf16)


def solution(mesh):
    sections, blocks, ranks = (mesh.shape[axis] for axis in ("sect", "dp", "tp"))
    devices = mesh.devices.reshape(sections, blocks, ranks // 2, 2)
    fine = Mesh(devices, ("sect", "dp", "zhi", "core"))
    tp = ("zhi", "core")
    placed = (
        P("dp", "sect", tp, None),
        P("dp", "sect", tp, None, None),
        P("dp", "sect", tp, None, None),
        P("dp", "sect", tp, None),
        P("dp", "sect", tp, None),
        P("dp", "sect"),
        P("dp", ("sect",) + tp),
        P(None, ("sect",) + tp),
        P(),
        P(),
        P("dp", "sect", tp),
        P("dp", "sect", tp),
        P("dp", tp, "sect"),
        P("dp", None),
    )
    return jax.shard_map(
        per_device, mesh=fine, in_specs=placed, out_specs=P("dp", ("sect",) + tp), check_vma=False
    )
```

```python
import math

import jax
import jax.numpy as jnp
from jax import lax
from jax.experimental import pallas as pl
from jax.experimental.pallas import tpu as pltpu
from jax.sharding import Mesh
from jax.sharding import PartitionSpec as P

norm_epsilon = 1e-05
f32 = jnp.float32
bf16 = jnp.bfloat16
last_with_last = (((1,), (1,)), ((), ()))
LOW = 16
SLOT = 32
FAR = 64


def lane_pick(values, lane):
    at = lax.broadcasted_iota(jnp.int32, values.shape, 1)
    return jnp.sum(jnp.where(at == lane, values, 0.0), axis=1, keepdims=True)


def high_part(values):
    return values.astype(bf16).astype(f32)


def place(routes_ref, gain_ref, router_ref, side_ref, taken_ref):
    experts = router_ref.shape[0]
    half = side_ref.shape[1]
    width = half // 4
    share = 2 * half
    slots, tokens = taken_ref.shape
    capacity = slots // experts
    first = lax.axis_index("core") == 0
    at = pl.multiple_of(lax.axis_index("sect") * share, 128)
    gain = gain_ref[:, pl.ds(at, share)]
    router = router_ref[:, pl.ds(at, share)].astype(f32)
    for pair in range(4):
        here = slice(pair * width, (pair + 1) * width)
        even = slice(2 * pair * width, (2 * pair + 1) * width)
        odd = slice((2 * pair + 1) * width, (2 * pair + 2) * width)
        side_ref[0:experts, here] = jnp.where(first, router[:, even], router[:, odd])
        side_ref[experts : experts + 1, here] = jnp.where(first, gain[:, even], gain[:, odd])
    routes = routes_ref[...]
    expert = lax.broadcasted_iota(jnp.int32, (experts, tokens), 0)
    named = [jnp.where(expert == routes[k : k + 1], 1.0, 0.0) for k in range(2)]
    before = jnp.where(
        lax.broadcasted_iota(jnp.int32, (tokens, tokens), 0)
        < lax.broadcasted_iota(jnp.int32, (tokens, tokens), 1),
        1.0,
        0.0,
    )
    earlier = jnp.dot(
        (named[0] + named[1]).astype(bf16), before.astype(bf16), preferred_element_type=f32
    )
    row = lax.broadcasted_iota(jnp.int32, (slots, tokens), 0)
    taken = jnp.zeros((slots, tokens), f32)
    for k in range(2):
        slot = jnp.sum(named[k] * earlier, axis=0, keepdims=True).astype(jnp.int32)
        taken = jnp.where(row == routes[k : k + 1] * capacity + slot, 1.0, taken)
    taken_ref[...] = taken.astype(bf16)


def attend_kernel(*refs):
    sources, outs, scratch = refs[:11], refs[11:16], refs[16:]
    out_ref, weight_ref, residual_ref, side_ref, taken_ref = outs
    lengths, q_ref, k_ref, v_ref, nk_ref, nv_ref, routes_ref, gain_ref, router_ref, sems = scratch
    targets = (
        k_ref,
        q_ref,
        lengths,
        nk_ref,
        routes_ref,
        gain_ref,
        router_ref,
        v_ref,
        nv_ref,
        weight_ref,
        residual_ref,
    )
    copies = [
        pltpu.make_async_copy(source, target, sems.at[i])
        for i, (source, target) in enumerate(zip(sources, targets, strict=True))
    ]
    for copy in copies:
        copy.start()
    for copy in copies[4:7]:
        copy.wait()
    place(routes_ref, gain_ref, router_ref, side_ref, taken_ref)
    for copy in copies[:4]:
        copy.wait()
    heads, tokens, head_size = q_ref.shape
    slots = k_ref.shape[1]
    rows = heads * tokens
    columns = tokens * slots
    scale = 1.0 / math.sqrt(head_size)
    queries = q_ref[...]
    scores = (
        lax.dot_general(
            queries.reshape(rows, head_size),
            k_ref[...].reshape(columns, head_size),
            last_with_last,
            preferred_element_type=f32,
        )
        * scale
    )
    column = lax.broadcasted_iota(jnp.int32, (1, columns), 1)
    owner = jnp.full((1, columns), -1, jnp.int32)
    for token in range(tokens):
        inside = (column >= token * slots) & (column < token * slots + lengths[token])
        owner = jnp.where(inside, token, owner)
    row_token = lax.broadcasted_iota(jnp.int32, (rows, 1), 0) & (tokens - 1)
    scores = jnp.where(row_token == owner, scores, -1e30)
    fresh = (
        jnp.sum(
            queries.astype(f32) * nk_ref[...].astype(f32)[None], axis=-1, keepdims=True
        ).reshape(rows, 1)
        * scale
    )
    highest = jnp.maximum(jnp.max(scores, axis=1, keepdims=True), fresh)
    weights = jnp.exp(scores - highest)
    fresh_weight = jnp.exp(fresh - highest)
    inverse = 1.0 / (jnp.sum(weights, axis=1, keepdims=True) + fresh_weight)
    probs = (weights * inverse).astype(bf16)
    fresh_prob = high_part(fresh_weight * inverse)
    for copy in copies[7:9]:
        copy.wait()
    fresh_values = jnp.broadcast_to(
        nv_ref[...].astype(f32)[None], (heads, tokens, head_size)
    ).reshape(rows, head_size)
    attended = jnp.dot(probs, v_ref[...].reshape(columns, head_size), preferred_element_type=f32)
    attended = (attended + fresh_prob * fresh_values).astype(bf16)
    for head in range(heads):
        block = attended[head * tokens : (head + 1) * tokens]
        for target in range(out_ref.shape[0]):
            out_ref[target, :, head * head_size : (head + 1) * head_size] = block
    for copy in copies[9:]:
        copy.wait()


def project_kernel(*refs):
    own, near, far = refs[:4], refs[4], refs[5]
    other = [near] + [far.at[k] for k in range(3)]
    weight_ref, residual_ref, hidden_ref, copies_ref = refs[6:]
    core = lax.axis_index("core")
    section = lax.axis_index("sect")
    ranks, tokens, width = own[0].shape
    total = None
    for rank in range(ranks):
        for pieces, odd in ((own, core), (other, 1 - core)):
            rows = jnp.concatenate([piece[rank] for piece in pieces], axis=0)
            at = pl.multiple_of((2 * rank + odd) * width, 128)
            product = lax.dot_general(
                rows, weight_ref[:, pl.ds(at, width)], last_with_last, preferred_element_type=f32
            )
            total = product if total is None else total + product
    for k in range(len(own)):
        at = pl.multiple_of(lax.rem(section + len(own) - k, len(own)) * tokens, tokens)
        hidden = residual_ref[pl.ds(at, tokens), :].astype(f32) + total[k * tokens : (k + 1) * tokens]
        hidden_ref[pl.ds(at, tokens), :] = hidden.astype(bf16)
    for target in range(copies_ref.shape[0]):
        copies_ref[target] = hidden_ref[...]


def dispatch_kernel(half_ref, side_ref, taken_ref, out_ref, stats_ref, wide_ref):
    pairs, tokens, width = half_ref.shape
    experts = out_ref.shape[0]
    for pair in range(pairs):
        wide_ref[:, pair * width : (pair + 1) * width] = half_ref[pair].astype(f32)
    wide = wide_ref[...]
    squares = jnp.sum(wide * wide, axis=1, keepdims=True)
    logits = lax.dot_general(
        (wide * side_ref[experts : experts + 1, :]).astype(bf16),
        side_ref[0:experts, :].astype(bf16),
        last_with_last,
        preferred_element_type=f32,
    )
    stats_ref[...] = jnp.zeros(stats_ref.shape, f32)
    stats_ref[:, :experts] = logits
    stats_ref[:, experts : experts + 1] = squares
    rows = jnp.dot(taken_ref[...], wide.astype(bf16), preferred_element_type=f32)
    out_ref[...] = rows.astype(bf16).reshape(out_ref.shape)


def expand_kernel(
    own_ref, other_ref, own_stats, other_stats, gain_ref, gate_ref, up_ref, *rest, offsets
):
    outs, wide_ref, scaled_ref = rest[:-2], rest[-2], rest[-1]
    sections = 4
    blocks, capacity, half = own_ref.shape
    per = blocks // sections
    rows = per * capacity
    share = 2 * half
    hidden_units = gate_ref.shape[1]
    pairs = 4
    width = half // pairs
    first = lax.axis_index("core") == 0
    section = lax.axis_index("sect")
    for k, offset in enumerate(offsets):
        at = lax.rem(section + jnp.where(first, offset[0], offset[1]), sections) * per
        own = own_ref[pl.ds(at, per)].astype(f32).reshape(rows, half)
        other = other_ref[pl.ds(at, per)].astype(f32).reshape(rows, half)
        for pair in range(pairs):
            mine = own[:, pair * width : (pair + 1) * width]
            theirs = other[:, pair * width : (pair + 1) * width]
            even = 2 * pair * width
            odd = even + width
            wide_ref[k * rows : (k + 1) * rows, even:odd] = jnp.where(first, mine, theirs)
            wide_ref[k * rows : (k + 1) * rows, odd : odd + width] = jnp.where(first, theirs, mine)
    gain = gain_ref[:, pl.ds(pl.multiple_of(section * share, 128), share)]
    stats = own_stats[...] + other_stats[...]
    high = high_part(stats)
    stats = high + pltpu.roll(stats - high, LOW, 1)
    lane = lax.broadcasted_iota(jnp.int32, (rows, 128), 1)
    for k in range(len(offsets)):
        x = wide_ref[k * rows : (k + 1) * rows, :]
        squares = jnp.sum(x * x, axis=1, keepdims=True)
        scaled_ref[k * rows : (k + 1) * rows, :] = (x * gain).astype(bf16)
        high = high_part(squares)
        extra = jnp.where(lane == SLOT, high, jnp.where(lane == SLOT + 1, squares - high, stats))
        outs[k][:, 2 * hidden_units :] = extra.astype(bf16)

    tile = 256

    def step(i, carry):
        at = pl.multiple_of(i * tile, tile)
        for which, weight_ref in enumerate((gate_ref, up_ref)):
            product = jnp.dot(
                scaled_ref[...], weight_ref[:, pl.ds(at, tile)], preferred_element_type=f32
            ).astype(bf16)
            target = pl.multiple_of(which * hidden_units + i * tile, tile)
            for k in range(len(offsets)):
                outs[k][:, pl.ds(target, tile)] = product[k * rows : (k + 1) * rows]
        return carry

    lax.fori_loop(0, hidden_units // tile, step, 0)


def relay_kernel(piece_ref, far_ref, out_ref):
    total = piece_ref.shape[1]
    products = slice(0, total - 128)
    stats = slice(total - 128, total)
    out_ref[:, products] = (
        piece_ref[:, products].astype(f32) + far_ref[:, products].astype(f32)
    ).astype(bf16)
    lane = lax.broadcasted_iota(jnp.int32, (piece_ref.shape[0], 128), 1)
    extra = jnp.where(
        lane < FAR, piece_ref[:, stats].astype(f32), pltpu.roll(far_ref[:, stats].astype(f32), FAR, 1)
    )
    out_ref[:, stats] = extra.astype(bf16)


def activate_kernel(*refs, features, capacity):
    parts, (routes_ref, out_ref, combine_ref) = refs[:3], refs[3:]
    tokens, hidden_units = out_ref.shape

    def summed(start, size):
        first, second, third = (part[:, start : start + size].astype(f32) for part in parts)
        return first + second + third

    stats = summed(2 * hidden_units, 128)
    stats = stats + pltpu.roll(stats, 128 - FAR, 1)
    slot_squares = lane_pick(stats, SLOT) + lane_pick(stats, SLOT + 1)
    slot_scale = lax.rsqrt(slot_squares * (1.0 / features) + norm_epsilon)
    gate = summed(0, hidden_units) * slot_scale
    up = summed(hidden_units, hidden_units) * slot_scale
    out_ref[...] = (gate / (1.0 + jnp.exp(-gate)) * up).astype(bf16)

    experts = combine_ref.shape[1] // capacity
    lane = lax.broadcasted_iota(jnp.int32, (tokens, 128), 1)
    full = stats + pltpu.roll(stats, 128 - LOW, 1)
    token_scale = lax.rsqrt(lane_pick(full, experts) * (1.0 / features) + norm_epsilon)
    at_row = lax.broadcasted_iota(jnp.int32, (tokens, tokens), 0)
    at_lane = lax.broadcasted_iota(jnp.int32, (tokens, tokens), 1)
    before = jnp.where(at_lane < at_row, 1.0, 0.0)
    route = [
        jnp.sum(
            jnp.where(at_row == at_lane, routes_ref[k : k + 1, :].astype(f32), 0.0),
            axis=1,
            keepdims=True,
        ).astype(jnp.int32)
        for k in range(2)
    ]
    named = [jnp.where(lane == route[k], 1.0, 0.0) for k in range(2)]
    earlier = jnp.dot(
        before.astype(bf16), (named[0] + named[1]).astype(bf16), preferred_element_type=f32
    )
    chosen = [jnp.sum(named[k] * full, axis=1, keepdims=True) * token_scale for k in range(2)]
    column = lax.broadcasted_iota(jnp.int32, combine_ref.shape, 1)
    combine = jnp.zeros(combine_ref.shape, f32)
    for k in range(2):
        slot = jnp.sum(named[k] * earlier, axis=1, keepdims=True).astype(jnp.int32)
        mixing = 1.0 / (1.0 + jnp.exp(chosen[1 - k] - chosen[k]))
        combine = jnp.where(column == route[k] * capacity + slot, mixing, combine)
    combine_ref[...] = combine


def contract_kernel(a0_ref, a1_ref, a2_ref, a3_ref, weight_ref, keep_ref, give_ref, rows_ref, give_wide):
    pieces = (a0_ref, a1_ref, a2_ref, a3_ref)
    rows = a0_ref.shape[0]
    blocks, capacity, half = keep_ref.shape
    pairs = 4
    width = half // pairs
    first = lax.axis_index("core") == 0
    section = lax.axis_index("sect")
    for k, piece in enumerate(pieces):
        rows_ref[lax.rem(section + len(pieces) - k, len(pieces))] = piece[...]
    full = rows_ref[...].reshape(len(pieces) * rows, rows_ref.shape[2])
    for chunk in range(2):
        product = jnp.dot(
            full, weight_ref[:, chunk * half : (chunk + 1) * half], preferred_element_type=f32
        )
        for pair in range(pairs // 2):
            even = product[:, 2 * pair * width : (2 * pair + 1) * width]
            odd = product[:, (2 * pair + 1) * width : (2 * pair + 2) * width]
            at = (chunk * (pairs // 2) + pair) * width
            kept = jnp.where(first, even, odd)
            keep_ref[:, :, at : at + width] = kept.reshape(blocks, capacity, width)
            give_wide[:, at : at + width] = jnp.where(first, odd, even)
    give_ref[...] = give_wide[...].astype(bf16).reshape(give_ref.shape)


def combine_kernel(y_ref, combine_ref, out_ref, wide_ref):
    pairs, tokens, width = out_ref.shape
    y = y_ref[...].reshape(combine_ref.shape[1], y_ref.shape[2])
    combine = combine_ref[...]
    high = combine.astype(bf16)
    low = (combine - high.astype(f32)).astype(bf16)
    wide_ref[...] = jnp.dot(high, y, preferred_element_type=f32) + jnp.dot(
        low, y, preferred_element_type=f32
    )
    for pair in range(pairs):
        out_ref[pair] = wide_ref[:, pair * width : (pair + 1) * width].astype(bf16)


def exchange(values, axis):
    return lax.all_to_all(values, axis, split_axis=0, concat_axis=0, tiled=True)


def swap(values):
    return lax.ppermute(values, "core", [(0, 1), (1, 0)])


def around(pieces):
    sections = len(pieces)
    arrived = list(pieces)
    for k in (2, 1, 3):
        arrived[k] = lax.ppermute(
            pieces[k], "sect", [(i, (i + k) % sections) for i in range(sections)]
        )
    return arrived


def call(kernel, name, out_shape, in_specs=None, scratch_shapes=()):
    extra = {} if in_specs is None else {"in_specs": in_specs}
    return pl.pallas_call(
        kernel,
        out_shape=out_shape,
        scratch_shapes=scratch_shapes,
        compiler_params=pltpu.CompilerParams(vmem_limit_bytes=16 << 20),
        name=name,
        **extra,
    )


def per_device(
    queries,
    key_cache,
    cached_values,
    incoming_keys,
    incoming_values,
    lengths,
    residual,
    out_proj,
    norm_gain,
    router,
    gate_proj,
    up_proj,
    down_proj,
    routes,
):
    sections = lax.axis_size("sect")
    ranks = lax.axis_size("zhi")
    _, tokens, heads, head_size = queries.shape
    slots = key_cache.shape[3]
    width = heads * head_size
    group, columns = residual.shape
    experts = router.shape[1]
    capacity = group // 2
    features = norm_gain.shape[0]
    half = features // sections // 2
    hidden_units = gate_proj.shape[2]
    rows = experts * capacity // sections
    struct = jax.ShapeDtypeStruct
    vmem = pltpu.VMEM

    gain = norm_gain.reshape(1, features)
    operands = (
        key_cache.reshape(tokens, slots, head_size),
        jnp.swapaxes(queries[0], 0, 1),
        lengths[0],
        incoming_keys.reshape(tokens, head_size),
        routes.T,
        gain,
        router.T,
        cached_values.reshape(tokens, slots, head_size),
        incoming_values.reshape(tokens, head_size),
        out_proj.T,
        residual,
    )
    attended, weight, residual, side, taken = call(
        attend_kernel,
        "attend",
        [
            struct((ranks, tokens, width), bf16),
            struct((columns, features), bf16),
            struct((group, columns), bf16),
            struct((2 * experts, half), f32),
            struct((experts * capacity, group), bf16),
        ],
        [pl.BlockSpec(memory_space=pltpu.HBM)] * len(operands),
        [
            pltpu.SMEM((tokens,), jnp.int32),
            vmem((heads, tokens, head_size), bf16),
            vmem((tokens, slots, head_size), bf16),
            vmem((tokens, slots, head_size), bf16),
            vmem((tokens, head_size), bf16),
            vmem((tokens, head_size), bf16),
            vmem((2, group), jnp.int32),
            vmem((1, features), f32),
            vmem((experts, features), bf16),
            pltpu.SemaphoreType.DMA((len(operands),)),
        ],
    )(*(pltpu.with_memory_space_constraint(operand, pltpu.HBM) for operand in operands))
    own = around([exchange(attended, "zhi")] * sections)
    other = [swap(own[0]), swap(jnp.stack(own[1:]))]
    hidden, copies = call(
        project_kernel,
        "project",
        [struct((group, columns), bf16), struct((ranks, group, columns), bf16)],
    )(*own, *other, weight, residual)

    outgoing, stats = call(
        dispatch_kernel,
        "dispatch",
        [struct((experts, capacity, half), bf16), struct((group, 128), f32)],
        None,
        [vmem((group, half), f32)],
    )(exchange(copies, "zhi"), side, taken)
    other_stats = swap(stats)
    arrived = exchange(outgoing, "dp")
    expand_operands = (arrived, swap(arrived), stats, other_stats, gain, gate_proj[0], up_proj[0])

    def expand(name, offsets):
        def kernel(*refs):
            expand_kernel(*refs, offsets=offsets)

        count = len(offsets) * rows
        return call(
            kernel,
            name,
            [struct((rows, 2 * hidden_units + 128), bf16)] * len(offsets),
            None,
            [vmem((count, 2 * half), f32), vmem((count, 2 * half), bf16)],
        )(*expand_operands)

    def outward(values, by):
        pairs = []
        for i in range(sections):
            pairs += [(2 * i, 2 * ((i + by) % sections)), (2 * i + 1, 2 * ((i - by) % sections) + 1)]
        return lax.ppermute(values, ("sect", "core"), pairs)

    (far,) = expand("expand_far", ((2, 2),))
    far = outward(far, 1)
    kept, direct, passed = expand("expand_near", ((0, 0), (3, 1), (1, 3)))
    direct = outward(direct, -1)
    passed = call(relay_kernel, "relay", struct((rows, 2 * hidden_units + 128), bf16))(passed, far)

    def activate(*refs):
        activate_kernel(*refs, features=features, capacity=capacity)

    activated, combine = call(
        activate,
        "activate",
        [struct((rows, hidden_units), bf16), struct((group, experts * capacity), f32)],
    )(kept, direct, outward(passed, 1), routes.T)

    keep, give = call(
        contract_kernel,
        "contract",
        [struct((experts, capacity, half), f32), struct((experts, capacity, half), bf16)],
        None,
        [vmem((sections, rows, hidden_units), bf16), vmem((experts * capacity, half), f32)],
    )(*around([activated] * sections), down_proj[0])
    outputs = (keep + swap(give).astype(f32)).astype(bf16)

    mixed = call(
        combine_kernel,
        "combine",
        struct((ranks, group, columns), bf16),
        None,
        [vmem((group, half), f32)],
    )(exchange(outputs, "dp"), combine)
    last = exchange(mixed, "zhi").astype(f32)
    return (hidden.astype(f32) + jnp.sum(last, axis=0)).astype(bf16)


def solution(mesh):
    sections, blocks, ranks = (mesh.shape[axis] for axis in ("sect", "dp", "tp"))
    devices = mesh.devices.reshape(sections, blocks, ranks // 2, 2)
    fine = Mesh(devices, ("sect", "dp", "zhi", "core"))
    tp = ("zhi", "core")
    placed = (
        P("dp", "sect", tp, None),
        P("dp", "sect", tp, None, None),
        P("dp", "sect", tp, None, None),
        P("dp", "sect", tp, None),
        P("dp", "sect", tp, None),
        P("dp", "sect"),
        P("dp", ("sect",) + tp),
        P(None, ("sect",) + tp),
        P(),
        P(),
        P("dp", "sect", tp),
        P("dp", "sect", tp),
        P("dp", tp, "sect"),
        P("dp", None),
    )
    return jax.shard_map(
        per_device, mesh=fine, in_specs=placed, out_specs=P("dp", ("sect",) + tp), check_vma=False
    )
```

```python
import math

import jax
import jax.numpy as jnp
from jax import lax
from jax.experimental import pallas as pl
from jax.experimental.pallas import tpu as pltpu
from jax.sharding import Mesh
from jax.sharding import PartitionSpec as P

norm_epsilon = 1e-05
f32 = jnp.float32
bf16 = jnp.bfloat16
last_with_last = (((1,), (1,)), ((), ()))
LOW = 16
SLOT = 32
FAR = 64


def lane_pick(values, lane):
    at = lax.broadcasted_iota(jnp.int32, values.shape, 1)
    return jnp.sum(jnp.where(at == lane, values, 0.0), axis=1, keepdims=True)


def high_part(values):
    return values.astype(bf16).astype(f32)


def place(routes_ref, gain_ref, router_ref, side_ref, taken_ref):
    experts = router_ref.shape[0]
    half = side_ref.shape[1]
    width = half // 4
    share = 2 * half
    slots, tokens = taken_ref.shape
    capacity = slots // experts
    first = lax.axis_index("core") == 0
    at = pl.multiple_of(lax.axis_index("sect") * share, 128)
    gain = gain_ref[:, pl.ds(at, share)]
    router = router_ref[:, pl.ds(at, share)].astype(f32)
    for pair in range(4):
        here = slice(pair * width, (pair + 1) * width)
        even = slice(2 * pair * width, (2 * pair + 1) * width)
        odd = slice((2 * pair + 1) * width, (2 * pair + 2) * width)
        side_ref[0:experts, here] = jnp.where(first, router[:, even], router[:, odd])
        side_ref[experts : experts + 1, here] = jnp.where(first, gain[:, even], gain[:, odd])
    routes = routes_ref[...]
    expert = lax.broadcasted_iota(jnp.int32, (experts, tokens), 0)
    named = [jnp.where(expert == routes[k : k + 1], 1.0, 0.0) for k in range(2)]
    before = jnp.where(
        lax.broadcasted_iota(jnp.int32, (tokens, tokens), 0)
        < lax.broadcasted_iota(jnp.int32, (tokens, tokens), 1),
        1.0,
        0.0,
    )
    earlier = jnp.dot(
        (named[0] + named[1]).astype(bf16), before.astype(bf16), preferred_element_type=f32
    )
    row = lax.broadcasted_iota(jnp.int32, (slots, tokens), 0)
    taken = jnp.zeros((slots, tokens), f32)
    for k in range(2):
        slot = jnp.sum(named[k] * earlier, axis=0, keepdims=True).astype(jnp.int32)
        taken = jnp.where(row == routes[k : k + 1] * capacity + slot, 1.0, taken)
    taken_ref[...] = taken.astype(bf16)


def attend_kernel(*refs):
    sources, outs, scratch = refs[:11], refs[11:16], refs[16:]
    out_ref, weight_ref, residual_ref, side_ref, taken_ref = outs
    lengths, q_ref, k_ref, v_ref, nk_ref, nv_ref, routes_ref, gain_ref, router_ref, sems = scratch
    targets = (
        k_ref,
        q_ref,
        lengths,
        nk_ref,
        routes_ref,
        gain_ref,
        router_ref,
        v_ref,
        nv_ref,
        weight_ref,
        residual_ref,
    )
    copies = [
        pltpu.make_async_copy(source, target, sems.at[i])
        for i, (source, target) in enumerate(zip(sources, targets, strict=True))
    ]
    for copy in copies:
        copy.start()
    for copy in copies[4:7]:
        copy.wait()
    place(routes_ref, gain_ref, router_ref, side_ref, taken_ref)
    for copy in copies[:4]:
        copy.wait()
    heads, tokens, head_size = q_ref.shape
    slots = k_ref.shape[1]
    rows = heads * tokens
    columns = tokens * slots
    scale = 1.0 / math.sqrt(head_size)
    queries = q_ref[...]
    scores = (
        lax.dot_general(
            queries.reshape(rows, head_size),
            k_ref[...].reshape(columns, head_size),
            last_with_last,
            preferred_element_type=f32,
        )
        * scale
    )
    column = lax.broadcasted_iota(jnp.int32, (1, columns), 1)
    owner = jnp.full((1, columns), -1, jnp.int32)
    for token in range(tokens):
        inside = (column >= token * slots) & (column < token * slots + lengths[token])
        owner = jnp.where(inside, token, owner)
    row_token = lax.broadcasted_iota(jnp.int32, (rows, 1), 0) & (tokens - 1)
    scores = jnp.where(row_token == owner, scores, -1e30)
    fresh = (
        jnp.sum(
            queries.astype(f32) * nk_ref[...].astype(f32)[None], axis=-1, keepdims=True
        ).reshape(rows, 1)
        * scale
    )
    highest = jnp.maximum(jnp.max(scores, axis=1, keepdims=True), fresh)
    weights = jnp.exp(scores - highest)
    fresh_weight = jnp.exp(fresh - highest)
    inverse = 1.0 / (jnp.sum(weights, axis=1, keepdims=True) + fresh_weight)
    probs = (weights * inverse).astype(bf16)
    fresh_prob = high_part(fresh_weight * inverse)
    for copy in copies[7:9]:
        copy.wait()
    fresh_values = jnp.broadcast_to(
        nv_ref[...].astype(f32)[None], (heads, tokens, head_size)
    ).reshape(rows, head_size)
    attended = jnp.dot(probs, v_ref[...].reshape(columns, head_size), preferred_element_type=f32)
    attended = (attended + fresh_prob * fresh_values).astype(bf16)
    for head in range(heads):
        block = attended[head * tokens : (head + 1) * tokens]
        out_ref[:, head * head_size : (head + 1) * head_size] = block
    for copy in copies[9:]:
        copy.wait()


def head_products(pieces, weight_ref, core):
    ranks, _, width = pieces[0].shape
    total = None
    for rank in range(ranks):
        rows = jnp.concatenate([piece[rank] for piece in pieces], axis=0)
        source = lax.rem(lax.axis_index("zhi") + ranks - rank, ranks)
        at = pl.multiple_of((2 * source + core) * width, 128)
        product = lax.dot_general(
            rows, weight_ref[:, pl.ds(at, width)], last_with_last, preferred_element_type=f32
        )
        total = product if total is None else total + product
    return total


def project_own_kernel(*refs):
    pieces, (weight_ref, total_ref) = refs[:4], refs[4:]
    total_ref[...] = head_products(pieces, weight_ref, lax.axis_index("core"))


def project_kernel(near, far, total_ref, weight_ref, residual_ref, hidden_ref):
    other = [near] + [far.at[k] for k in range(3)]
    section = lax.axis_index("sect")
    tokens = near.shape[1]
    total = total_ref[...] + head_products(other, weight_ref, 1 - lax.axis_index("core"))
    for k in range(len(other)):
        at = pl.multiple_of(lax.rem(section + len(other) - k, len(other)) * tokens, tokens)
        hidden = residual_ref[pl.ds(at, tokens), :].astype(f32) + total[k * tokens : (k + 1) * tokens]
        hidden_ref[pl.ds(at, tokens), :] = hidden.astype(bf16)


def dispatch_kernel(*refs):
    pieces, (side_ref, taken_ref, out_ref, stats_ref, half_ref, wide_ref) = refs[:4], refs[4:]
    pairs, tokens, width = half_ref.shape
    experts = out_ref.shape[0]
    rank = lax.axis_index("zhi")
    for k, piece in enumerate(pieces):
        half_ref[lax.rem(rank + pairs - k, pairs)] = piece[...]
    for pair in range(pairs):
        wide_ref[:, pair * width : (pair + 1) * width] = half_ref[pair].astype(f32)
    wide = wide_ref[...]
    squares = jnp.sum(wide * wide, axis=1, keepdims=True)
    logits = lax.dot_general(
        (wide * side_ref[experts : experts + 1, :]).astype(bf16),
        side_ref[0:experts, :].astype(bf16),
        last_with_last,
        preferred_element_type=f32,
    )
    stats_ref[...] = jnp.zeros(stats_ref.shape, f32)
    stats_ref[:, :experts] = logits
    stats_ref[:, experts : experts + 1] = squares
    rows = jnp.dot(taken_ref[...], wide.astype(bf16), preferred_element_type=f32)
    out_ref[...] = rows.astype(bf16).reshape(out_ref.shape)


def expand_kernel(
    own_ref, other_ref, own_stats, other_stats, gain_ref, gate_ref, up_ref, *rest, offsets
):
    outs, wide_ref, scaled_ref = rest[:-2], rest[-2], rest[-1]
    sections = 4
    blocks, capacity, half = own_ref.shape
    per = blocks // sections
    rows = per * capacity
    share = 2 * half
    hidden_units = gate_ref.shape[1]
    pairs = 4
    width = half // pairs
    first = lax.axis_index("core") == 0
    section = lax.axis_index("sect")
    for k, offset in enumerate(offsets):
        at = lax.rem(section + jnp.where(first, offset[0], offset[1]), sections) * per
        own = own_ref[pl.ds(at, per)].astype(f32).reshape(rows, half)
        other = other_ref[pl.ds(at, per)].astype(f32).reshape(rows, half)
        for pair in range(pairs):
            mine = own[:, pair * width : (pair + 1) * width]
            theirs = other[:, pair * width : (pair + 1) * width]
            even = 2 * pair * width
            odd = even + width
            wide_ref[k * rows : (k + 1) * rows, even:odd] = jnp.where(first, mine, theirs)
            wide_ref[k * rows : (k + 1) * rows, odd : odd + width] = jnp.where(first, theirs, mine)
    gain = gain_ref[:, pl.ds(pl.multiple_of(section * share, 128), share)]
    stats = own_stats[...] + other_stats[...]
    high = high_part(stats)
    stats = high + pltpu.roll(stats - high, LOW, 1)
    lane = lax.broadcasted_iota(jnp.int32, (rows, 128), 1)
    for k in range(len(offsets)):
        x = wide_ref[k * rows : (k + 1) * rows, :]
        squares = jnp.sum(x * x, axis=1, keepdims=True)
        scaled_ref[k * rows : (k + 1) * rows, :] = (x * gain).astype(bf16)
        high = high_part(squares)
        extra = jnp.where(lane == SLOT, high, jnp.where(lane == SLOT + 1, squares - high, stats))
        outs[k][:, 2 * hidden_units :] = extra.astype(bf16)

    tile = 256

    def step(i, carry):
        at = pl.multiple_of(i * tile, tile)
        for which, weight_ref in enumerate((gate_ref, up_ref)):
            product = jnp.dot(
                scaled_ref[...], weight_ref[:, pl.ds(at, tile)], preferred_element_type=f32
            ).astype(bf16)
            target = pl.multiple_of(which * hidden_units + i * tile, tile)
            for k in range(len(offsets)):
                outs[k][:, pl.ds(target, tile)] = product[k * rows : (k + 1) * rows]
        return carry

    lax.fori_loop(0, hidden_units // tile, step, 0)


def relay_kernel(piece_ref, far_ref, out_ref):
    total = piece_ref.shape[1]
    products = slice(0, total - 128)
    stats = slice(total - 128, total)
    out_ref[:, products] = (
        piece_ref[:, products].astype(f32) + far_ref[:, products].astype(f32)
    ).astype(bf16)
    lane = lax.broadcasted_iota(jnp.int32, (piece_ref.shape[0], 128), 1)
    extra = jnp.where(
        lane < FAR, piece_ref[:, stats].astype(f32), pltpu.roll(far_ref[:, stats].astype(f32), FAR, 1)
    )
    out_ref[:, stats] = extra.astype(bf16)


def activate_kernel(*refs, features, capacity):
    parts, (routes_ref, out_ref, combine_ref) = refs[:3], refs[3:]
    tokens, hidden_units = out_ref.shape

    def summed(start, size):
        first, second, third = (part[:, start : start + size].astype(f32) for part in parts)
        return first + second + third

    stats = summed(2 * hidden_units, 128)
    stats = stats + pltpu.roll(stats, 128 - FAR, 1)
    slot_squares = lane_pick(stats, SLOT) + lane_pick(stats, SLOT + 1)
    slot_scale = lax.rsqrt(slot_squares * (1.0 / features) + norm_epsilon)
    gate = summed(0, hidden_units) * slot_scale
    up = summed(hidden_units, hidden_units) * slot_scale
    out_ref[...] = (gate / (1.0 + jnp.exp(-gate)) * up).astype(bf16)

    experts = combine_ref.shape[1] // capacity
    lane = lax.broadcasted_iota(jnp.int32, (tokens, 128), 1)
    full = stats + pltpu.roll(stats, 128 - LOW, 1)
    token_scale = lax.rsqrt(lane_pick(full, experts) * (1.0 / features) + norm_epsilon)
    at_row = lax.broadcasted_iota(jnp.int32, (tokens, tokens), 0)
    at_lane = lax.broadcasted_iota(jnp.int32, (tokens, tokens), 1)
    before = jnp.where(at_lane < at_row, 1.0, 0.0)
    route = [
        jnp.sum(
            jnp.where(at_row == at_lane, routes_ref[k : k + 1, :].astype(f32), 0.0),
            axis=1,
            keepdims=True,
        ).astype(jnp.int32)
        for k in range(2)
    ]
    named = [jnp.where(lane == route[k], 1.0, 0.0) for k in range(2)]
    earlier = jnp.dot(
        before.astype(bf16), (named[0] + named[1]).astype(bf16), preferred_element_type=f32
    )
    chosen = [jnp.sum(named[k] * full, axis=1, keepdims=True) * token_scale for k in range(2)]
    column = lax.broadcasted_iota(jnp.int32, combine_ref.shape, 1)
    combine = jnp.zeros(combine_ref.shape, f32)
    for k in range(2):
        slot = jnp.sum(named[k] * earlier, axis=1, keepdims=True).astype(jnp.int32)
        mixing = 1.0 / (1.0 + jnp.exp(chosen[1 - k] - chosen[k]))
        combine = jnp.where(column == route[k] * capacity + slot, mixing, combine)
    combine_ref[...] = combine


def contract_kernel(a0_ref, a1_ref, a2_ref, a3_ref, weight_ref, keep_ref, give_ref, rows_ref, give_wide):
    pieces = (a0_ref, a1_ref, a2_ref, a3_ref)
    rows = a0_ref.shape[0]
    blocks, capacity, half = keep_ref.shape
    pairs = 4
    width = half // pairs
    first = lax.axis_index("core") == 0
    section = lax.axis_index("sect")
    for k, piece in enumerate(pieces):
        rows_ref[lax.rem(section + len(pieces) - k, len(pieces))] = piece[...]
    full = rows_ref[...].reshape(len(pieces) * rows, rows_ref.shape[2])
    for chunk in range(2):
        product = jnp.dot(
            full, weight_ref[:, chunk * half : (chunk + 1) * half], preferred_element_type=f32
        )
        for pair in range(pairs // 2):
            even = product[:, 2 * pair * width : (2 * pair + 1) * width]
            odd = product[:, (2 * pair + 1) * width : (2 * pair + 2) * width]
            at = (chunk * (pairs // 2) + pair) * width
            kept = jnp.where(first, even, odd)
            keep_ref[:, :, at : at + width] = kept.reshape(blocks, capacity, width)
            give_wide[:, at : at + width] = jnp.where(first, odd, even)
    give_ref[...] = give_wide[...].astype(bf16).reshape(give_ref.shape)


def combine_kernel(y_ref, combine_ref, *rest):
    outs, wide_ref, parts_ref = rest[:4], rest[4], rest[5]
    pairs, tokens, width = parts_ref.shape
    rank = lax.axis_index("zhi")
    y = y_ref[...].reshape(combine_ref.shape[1], y_ref.shape[2])
    combine = combine_ref[...]
    high = combine.astype(bf16)
    low = (combine - high.astype(f32)).astype(bf16)
    wide_ref[...] = jnp.dot(high, y, preferred_element_type=f32) + jnp.dot(
        low, y, preferred_element_type=f32
    )
    for pair in range(pairs):
        parts_ref[pair] = wide_ref[:, pair * width : (pair + 1) * width].astype(bf16)
    for k, out in enumerate(outs):
        out[...] = parts_ref[lax.rem(rank + k, pairs)]


def exchange(values, axis):
    return lax.all_to_all(values, axis, split_axis=0, concat_axis=0, tiled=True)


def swap(values):
    return lax.ppermute(values, "core", [(0, 1), (1, 0)])


def around(pieces, axis="sect"):
    count = len(pieces)
    arrived = list(pieces)
    for k in (2, 1, 3):
        arrived[k] = lax.ppermute(pieces[k], axis, [(i, (i + k) % count) for i in range(count)])
    return arrived


def call(kernel, name, out_shape, in_specs=None, scratch_shapes=()):
    extra = {} if in_specs is None else {"in_specs": in_specs}
    return pl.pallas_call(
        kernel,
        out_shape=out_shape,
        scratch_shapes=scratch_shapes,
        compiler_params=pltpu.CompilerParams(vmem_limit_bytes=16 << 20),
        name=name,
        **extra,
    )


def per_device(
    queries,
    key_cache,
    cached_values,
    incoming_keys,
    incoming_values,
    lengths,
    residual,
    out_proj,
    norm_gain,
    router,
    gate_proj,
    up_proj,
    down_proj,
    routes,
):
    sections = lax.axis_size("sect")
    ranks = lax.axis_size("zhi")
    _, tokens, heads, head_size = queries.shape
    slots = key_cache.shape[3]
    width = heads * head_size
    group, columns = residual.shape
    experts = router.shape[1]
    capacity = group // 2
    features = norm_gain.shape[0]
    half = features // sections // 2
    hidden_units = gate_proj.shape[2]
    rows = experts * capacity // sections
    struct = jax.ShapeDtypeStruct
    vmem = pltpu.VMEM

    gain = norm_gain.reshape(1, features)
    operands = (
        key_cache.reshape(tokens, slots, head_size),
        jnp.swapaxes(queries[0], 0, 1),
        lengths[0],
        incoming_keys.reshape(tokens, head_size),
        routes.T,
        gain,
        router.T,
        cached_values.reshape(tokens, slots, head_size),
        incoming_values.reshape(tokens, head_size),
        out_proj.T,
        residual,
    )
    attended, weight, residual, side, taken = call(
        attend_kernel,
        "attend",
        [
            struct((tokens, width), bf16),
            struct((columns, features), bf16),
            struct((group, columns), bf16),
            struct((2 * experts, half), f32),
            struct((experts * capacity, group), bf16),
        ],
        [pl.BlockSpec(memory_space=pltpu.HBM)] * len(operands),
        [
            pltpu.SMEM((tokens,), jnp.int32),
            vmem((heads, tokens, head_size), bf16),
            vmem((tokens, slots, head_size), bf16),
            vmem((tokens, slots, head_size), bf16),
            vmem((tokens, head_size), bf16),
            vmem((tokens, head_size), bf16),
            vmem((2, group), jnp.int32),
            vmem((1, features), f32),
            vmem((experts, features), bf16),
            pltpu.SemaphoreType.DMA((len(operands),)),
        ],
    )(*(pltpu.with_memory_space_constraint(operand, pltpu.HBM) for operand in operands))
    own = around([jnp.stack(around([attended] * ranks, "zhi"))] * sections)
    other = [swap(own[0]), swap(jnp.stack(own[1:]))]
    total = call(project_own_kernel, "project_own", struct((group, columns), f32))(*own, weight)
    hidden = call(project_kernel, "project", struct((group, columns), bf16))(
        *other, total, weight, residual
    )

    outgoing, stats = call(
        dispatch_kernel,
        "dispatch",
        [struct((experts, capacity, half), bf16), struct((group, 128), f32)],
        None,
        [vmem((ranks, group, columns), bf16), vmem((group, half), f32)],
    )(*around([hidden] * ranks, "zhi"), side, taken)
    other_stats = swap(stats)
    arrived = exchange(outgoing, "dp")
    expand_operands = (arrived, swap(arrived), stats, other_stats, gain, gate_proj[0], up_proj[0])

    def expand(name, offsets):
        def kernel(*refs):
            expand_kernel(*refs, offsets=offsets)

        count = len(offsets) * rows
        return call(
            kernel,
            name,
            [struct((rows, 2 * hidden_units + 128), bf16)] * len(offsets),
            None,
            [vmem((count, 2 * half), f32), vmem((count, 2 * half), bf16)],
        )(*expand_operands)

    def outward(values, by):
        pairs = []
        for i in range(sections):
            pairs += [(2 * i, 2 * ((i + by) % sections)), (2 * i + 1, 2 * ((i - by) % sections) + 1)]
        return lax.ppermute(values, ("sect", "core"), pairs)

    (far,) = expand("expand_far", ((2, 2),))
    far = outward(far, 1)
    kept, direct, passed = expand("expand_near", ((0, 0), (3, 1), (1, 3)))
    direct = outward(direct, -1)
    passed = call(relay_kernel, "relay", struct((rows, 2 * hidden_units + 128), bf16))(passed, far)

    def activate(*refs):
        activate_kernel(*refs, features=features, capacity=capacity)

    activated, combine = call(
        activate,
        "activate",
        [struct((rows, hidden_units), bf16), struct((group, experts * capacity), f32)],
    )(kept, direct, outward(passed, 1), routes.T)

    keep, give = call(
        contract_kernel,
        "contract",
        [struct((experts, capacity, half), f32), struct((experts, capacity, half), bf16)],
        None,
        [vmem((sections, rows, hidden_units), bf16), vmem((experts * capacity, half), f32)],
    )(*around([activated] * sections), down_proj[0])
    outputs = (keep + swap(give).astype(f32)).astype(bf16)

    mixed = call(
        combine_kernel,
        "combine",
        [struct((group, columns), bf16)] * ranks,
        None,
        [vmem((group, half), f32), vmem((ranks, group, columns), bf16)],
    )(exchange(outputs, "dp"), combine)
    total = hidden.astype(f32)
    for part in around(mixed, "zhi"):
        total = total + part.astype(f32)
    return total.astype(bf16)


def solution(mesh):
    sections, blocks, ranks = (mesh.shape[axis] for axis in ("sect", "dp", "tp"))
    devices = mesh.devices.reshape(sections, blocks, ranks // 2, 2)
    fine = Mesh(devices, ("sect", "dp", "zhi", "core"))
    tp = ("zhi", "core")
    placed = (
        P("dp", "sect", tp, None),
        P("dp", "sect", tp, None, None),
        P("dp", "sect", tp, None, None),
        P("dp", "sect", tp, None),
        P("dp", "sect", tp, None),
        P("dp", "sect"),
        P("dp", ("sect",) + tp),
        P(None, ("sect",) + tp),
        P(),
        P(),
        P("dp", "sect", tp),
        P("dp", "sect", tp),
        P("dp", tp, "sect"),
        P("dp", None),
    )
    return jax.shard_map(
        per_device, mesh=fine, in_specs=placed, out_specs=P("dp", ("sect",) + tp), check_vma=False
    )
```

```python
import math

import jax
import jax.numpy as jnp
from jax import lax
from jax.experimental import pallas as pl
from jax.experimental.pallas import tpu as pltpu
from jax.sharding import Mesh
from jax.sharding import PartitionSpec as P

norm_epsilon = 1e-05
f32 = jnp.float32
bf16 = jnp.bfloat16
last_with_last = (((1,), (1,)), ((), ()))
LOW = 16
SLOT = 32
FAR = 64


def lane_pick(values, lane):
    at = lax.broadcasted_iota(jnp.int32, values.shape, 1)
    return jnp.sum(jnp.where(at == lane, values, 0.0), axis=1, keepdims=True)


def high_part(values):
    return values.astype(bf16).astype(f32)


def place(routes_ref, gain_ref, router_ref, side_ref, taken_ref):
    experts = router_ref.shape[0]
    half = side_ref.shape[1]
    width = half // 4
    share = 2 * half
    slots, tokens = taken_ref.shape
    capacity = slots // experts
    first = lax.axis_index("core") == 0
    at = pl.multiple_of(lax.axis_index("sect") * share, 128)
    gain = gain_ref[:, pl.ds(at, share)]
    router = router_ref[:, pl.ds(at, share)].astype(f32)
    for pair in range(4):
        here = slice(pair * width, (pair + 1) * width)
        even = slice(2 * pair * width, (2 * pair + 1) * width)
        odd = slice((2 * pair + 1) * width, (2 * pair + 2) * width)
        side_ref[0:experts, here] = jnp.where(first, router[:, even], router[:, odd])
        side_ref[experts : experts + 1, here] = jnp.where(first, gain[:, even], gain[:, odd])
    routes = routes_ref[...]
    expert = lax.broadcasted_iota(jnp.int32, (experts, tokens), 0)
    named = [jnp.where(expert == routes[k : k + 1], 1.0, 0.0) for k in range(2)]
    before = jnp.where(
        lax.broadcasted_iota(jnp.int32, (tokens, tokens), 0)
        < lax.broadcasted_iota(jnp.int32, (tokens, tokens), 1),
        1.0,
        0.0,
    )
    earlier = jnp.dot(
        (named[0] + named[1]).astype(bf16), before.astype(bf16), preferred_element_type=f32
    )
    row = lax.broadcasted_iota(jnp.int32, (slots, tokens), 0)
    taken = jnp.zeros((slots, tokens), f32)
    for k in range(2):
        slot = jnp.sum(named[k] * earlier, axis=0, keepdims=True).astype(jnp.int32)
        taken = jnp.where(row == routes[k : k + 1] * capacity + slot, 1.0, taken)
    taken_ref[...] = taken.astype(bf16)


def attend_kernel(*refs):
    sources, outs, scratch = refs[:11], refs[11:16], refs[16:]
    out_ref, weight_ref, residual_ref, side_ref, taken_ref = outs
    lengths, q_ref, k_ref, v_ref, nk_ref, nv_ref, routes_ref, gain_ref, router_ref, sems = scratch
    targets = (
        k_ref,
        q_ref,
        lengths,
        nk_ref,
        routes_ref,
        gain_ref,
        router_ref,
        v_ref,
        nv_ref,
        weight_ref,
        residual_ref,
    )
    copies = [
        pltpu.make_async_copy(source, target, sems.at[i])
        for i, (source, target) in enumerate(zip(sources, targets, strict=True))
    ]
    for copy in copies:
        copy.start()
    for copy in copies[4:7]:
        copy.wait()
    place(routes_ref, gain_ref, router_ref, side_ref, taken_ref)
    for copy in copies[:4]:
        copy.wait()
    heads, tokens, head_size = q_ref.shape
    slots = k_ref.shape[1]
    rows = heads * tokens
    columns = tokens * slots
    scale = 1.0 / math.sqrt(head_size)
    queries = q_ref[...]
    scores = (
        lax.dot_general(
            queries.reshape(rows, head_size),
            k_ref[...].reshape(columns, head_size),
            last_with_last,
            preferred_element_type=f32,
        )
        * scale
    )
    column = lax.broadcasted_iota(jnp.int32, (1, columns), 1)
    owner = jnp.full((1, columns), -1, jnp.int32)
    for token in range(tokens):
        inside = (column >= token * slots) & (column < token * slots + lengths[token])
        owner = jnp.where(inside, token, owner)
    row_token = lax.broadcasted_iota(jnp.int32, (rows, 1), 0) & (tokens - 1)
    scores = jnp.where(row_token == owner, scores, -1e30)
    fresh = (
        jnp.sum(
            queries.astype(f32) * nk_ref[...].astype(f32)[None], axis=-1, keepdims=True
        ).reshape(rows, 1)
        * scale
    )
    highest = jnp.maximum(jnp.max(scores, axis=1, keepdims=True), fresh)
    weights = jnp.exp(scores - highest)
    fresh_weight = jnp.exp(fresh - highest)
    inverse = 1.0 / (jnp.sum(weights, axis=1, keepdims=True) + fresh_weight)
    probs = (weights * inverse).astype(bf16)
    fresh_prob = high_part(fresh_weight * inverse)
    for copy in copies[7:9]:
        copy.wait()
    fresh_values = jnp.broadcast_to(
        nv_ref[...].astype(f32)[None], (heads, tokens, head_size)
    ).reshape(rows, head_size)
    attended = jnp.dot(probs, v_ref[...].reshape(columns, head_size), preferred_element_type=f32)
    attended = (attended + fresh_prob * fresh_values).astype(bf16)
    for head in range(heads):
        block = attended[head * tokens : (head + 1) * tokens]
        out_ref[:, head * head_size : (head + 1) * head_size] = block
    for copy in copies[9:]:
        copy.wait()


def head_products(pieces, weight_ref, core):
    ranks, _, width = pieces[0].shape
    total = None
    for rank in range(ranks):
        rows = jnp.concatenate([piece[rank] for piece in pieces], axis=0)
        source = lax.rem(lax.axis_index("zhi") + ranks - rank, ranks)
        at = pl.multiple_of((2 * source + core) * width, 128)
        product = lax.dot_general(
            rows, weight_ref[:, pl.ds(at, width)], last_with_last, preferred_element_type=f32
        )
        total = product if total is None else total + product
    return total


def project_own_kernel(*refs):
    pieces, (weight_ref, total_ref) = refs[:4], refs[4:]
    total_ref[...] = head_products(pieces, weight_ref, lax.axis_index("core"))


def project_kernel(near, far, total_ref, weight_ref, residual_ref, hidden_ref):
    other = [near] + [far.at[k] for k in range(3)]
    section = lax.axis_index("sect")
    tokens = near.shape[1]
    total = total_ref[...] + head_products(other, weight_ref, 1 - lax.axis_index("core"))
    for k in range(len(other)):
        at = pl.multiple_of(lax.rem(section + len(other) - k, len(other)) * tokens, tokens)
        hidden = residual_ref[pl.ds(at, tokens), :].astype(f32) + total[k * tokens : (k + 1) * tokens]
        hidden_ref[pl.ds(at, tokens), :] = hidden.astype(bf16)


def dispatch_kernel(*refs):
    pieces, (side_ref, taken_ref, out_ref, stats_ref, half_ref, wide_ref) = refs[:4], refs[4:]
    pairs, tokens, width = half_ref.shape
    experts = out_ref.shape[0]
    rank = lax.axis_index("zhi")
    for k, piece in enumerate(pieces):
        half_ref[lax.rem(rank + pairs - k, pairs)] = piece[...]
    for pair in range(pairs):
        wide_ref[:, pair * width : (pair + 1) * width] = half_ref[pair].astype(f32)
    wide = wide_ref[...]
    squares = jnp.sum(wide * wide, axis=1, keepdims=True)
    logits = lax.dot_general(
        (wide * side_ref[experts : experts + 1, :]).astype(bf16),
        side_ref[0:experts, :].astype(bf16),
        last_with_last,
        preferred_element_type=f32,
    )
    stats_ref[...] = jnp.zeros(stats_ref.shape, f32)
    stats_ref[:, :experts] = logits
    stats_ref[:, experts : experts + 1] = squares
    rows = jnp.dot(taken_ref[...], wide.astype(bf16), preferred_element_type=f32)
    out_ref[...] = rows.astype(bf16).reshape(out_ref.shape)


def expand_kernel(
    own_ref, other_ref, own_stats, other_stats, gain_ref, gate_ref, up_ref, *rest, offsets
):
    outs, wide_ref, scaled_ref = rest[:-2], rest[-2], rest[-1]
    sections = 4
    blocks, capacity, half = own_ref.shape
    per = blocks // sections
    rows = per * capacity
    share = 2 * half
    hidden_units = gate_ref.shape[1]
    pairs = 4
    width = half // pairs
    first = lax.axis_index("core") == 0
    section = lax.axis_index("sect")
    for k, offset in enumerate(offsets):
        at = lax.rem(section + jnp.where(first, offset[0], offset[1]), sections) * per
        own = own_ref[pl.ds(at, per)].astype(f32).reshape(rows, half)
        other = other_ref[pl.ds(at, per)].astype(f32).reshape(rows, half)
        for pair in range(pairs):
            mine = own[:, pair * width : (pair + 1) * width]
            theirs = other[:, pair * width : (pair + 1) * width]
            even = 2 * pair * width
            odd = even + width
            wide_ref[k * rows : (k + 1) * rows, even:odd] = jnp.where(first, mine, theirs)
            wide_ref[k * rows : (k + 1) * rows, odd : odd + width] = jnp.where(first, theirs, mine)
    gain = gain_ref[:, pl.ds(pl.multiple_of(section * share, 128), share)]
    stats = own_stats[...] + other_stats[...]
    high = high_part(stats)
    stats = high + pltpu.roll(stats - high, LOW, 1)
    lane = lax.broadcasted_iota(jnp.int32, (rows, 128), 1)
    for k in range(len(offsets)):
        x = wide_ref[k * rows : (k + 1) * rows, :]
        squares = jnp.sum(x * x, axis=1, keepdims=True)
        scaled_ref[k * rows : (k + 1) * rows, :] = (x * gain).astype(bf16)
        high = high_part(squares)
        extra = jnp.where(lane == SLOT, high, jnp.where(lane == SLOT + 1, squares - high, stats))
        outs[k][:, 2 * hidden_units :] = extra.astype(bf16)

    tile = 1024

    def step(i, carry):
        at = pl.multiple_of(i * tile, tile)
        for which, weight_ref in enumerate((gate_ref, up_ref)):
            product = jnp.dot(
                scaled_ref[...], weight_ref[:, pl.ds(at, tile)], preferred_element_type=f32
            ).astype(bf16)
            target = pl.multiple_of(which * hidden_units + i * tile, tile)
            for k in range(len(offsets)):
                outs[k][:, pl.ds(target, tile)] = product[k * rows : (k + 1) * rows]
        return carry

    lax.fori_loop(0, hidden_units // tile, step, 0)


def relay_kernel(piece_ref, far_ref, out_ref):
    total = piece_ref.shape[1]
    products = slice(0, total - 128)
    stats = slice(total - 128, total)
    out_ref[:, products] = (
        piece_ref[:, products].astype(f32) + far_ref[:, products].astype(f32)
    ).astype(bf16)
    lane = lax.broadcasted_iota(jnp.int32, (piece_ref.shape[0], 128), 1)
    extra = jnp.where(
        lane < FAR, piece_ref[:, stats].astype(f32), pltpu.roll(far_ref[:, stats].astype(f32), FAR, 1)
    )
    out_ref[:, stats] = extra.astype(bf16)


def activate_kernel(*refs, features, capacity):
    parts, (routes_ref, out_ref, combine_ref) = refs[:3], refs[3:]
    tokens, hidden_units = out_ref.shape

    def summed(start, size):
        first, second, third = (part[:, start : start + size].astype(f32) for part in parts)
        return first + second + third

    stats = summed(2 * hidden_units, 128)
    stats = stats + pltpu.roll(stats, 128 - FAR, 1)
    slot_squares = lane_pick(stats, SLOT) + lane_pick(stats, SLOT + 1)
    slot_scale = lax.rsqrt(slot_squares * (1.0 / features) + norm_epsilon)
    gate = summed(0, hidden_units) * slot_scale
    up = summed(hidden_units, hidden_units) * slot_scale
    out_ref[...] = (gate / (1.0 + jnp.exp(-gate)) * up).astype(bf16)

    experts = combine_ref.shape[1] // capacity
    lane = lax.broadcasted_iota(jnp.int32, (tokens, 128), 1)
    full = stats + pltpu.roll(stats, 128 - LOW, 1)
    token_scale = lax.rsqrt(lane_pick(full, experts) * (1.0 / features) + norm_epsilon)
    at_row = lax.broadcasted_iota(jnp.int32, (tokens, tokens), 0)
    at_lane = lax.broadcasted_iota(jnp.int32, (tokens, tokens), 1)
    before = jnp.where(at_lane < at_row, 1.0, 0.0)
    route = [
        jnp.sum(
            jnp.where(at_row == at_lane, routes_ref[k : k + 1, :].astype(f32), 0.0),
            axis=1,
            keepdims=True,
        ).astype(jnp.int32)
        for k in range(2)
    ]
    named = [jnp.where(lane == route[k], 1.0, 0.0) for k in range(2)]
    earlier = jnp.dot(
        before.astype(bf16), (named[0] + named[1]).astype(bf16), preferred_element_type=f32
    )
    chosen = [jnp.sum(named[k] * full, axis=1, keepdims=True) * token_scale for k in range(2)]
    column = lax.broadcasted_iota(jnp.int32, combine_ref.shape, 1)
    combine = jnp.zeros(combine_ref.shape, f32)
    for k in range(2):
        slot = jnp.sum(named[k] * earlier, axis=1, keepdims=True).astype(jnp.int32)
        mixing = 1.0 / (1.0 + jnp.exp(chosen[1 - k] - chosen[k]))
        combine = jnp.where(column == route[k] * capacity + slot, mixing, combine)
    combine_ref[...] = combine


def contract_kernel(a0_ref, a1_ref, a2_ref, a3_ref, weight_ref, keep_ref, give_ref, rows_ref, give_wide):
    pieces = (a0_ref, a1_ref, a2_ref, a3_ref)
    rows = a0_ref.shape[0]
    blocks, capacity, half = keep_ref.shape
    pairs = 4
    width = half // pairs
    first = lax.axis_index("core") == 0
    section = lax.axis_index("sect")
    for k, piece in enumerate(pieces):
        rows_ref[lax.rem(section + len(pieces) - k, len(pieces))] = piece[...]
    full = rows_ref[...].reshape(len(pieces) * rows, rows_ref.shape[2])
    for chunk in range(2):
        product = jnp.dot(
            full, weight_ref[:, chunk * half : (chunk + 1) * half], preferred_element_type=f32
        )
        for pair in range(pairs // 2):
            even = product[:, 2 * pair * width : (2 * pair + 1) * width]
            odd = product[:, (2 * pair + 1) * width : (2 * pair + 2) * width]
            at = (chunk * (pairs // 2) + pair) * width
            kept = jnp.where(first, even, odd)
            keep_ref[:, :, at : at + width] = kept.reshape(blocks, capacity, width)
            give_wide[:, at : at + width] = jnp.where(first, odd, even)
    give_ref[...] = give_wide[...].astype(bf16).reshape(give_ref.shape)


def combine_kernel(y_ref, combine_ref, *rest):
    outs, wide_ref, parts_ref = rest[:4], rest[4], rest[5]
    pairs, tokens, width = parts_ref.shape
    rank = lax.axis_index("zhi")
    y = y_ref[...].reshape(combine_ref.shape[1], y_ref.shape[2])
    combine = combine_ref[...]
    high = combine.astype(bf16)
    low = (combine - high.astype(f32)).astype(bf16)
    wide_ref[...] = jnp.dot(high, y, preferred_element_type=f32) + jnp.dot(
        low, y, preferred_element_type=f32
    )
    for pair in range(pairs):
        parts_ref[pair] = wide_ref[:, pair * width : (pair + 1) * width].astype(bf16)
    for k, out in enumerate(outs):
        out[...] = parts_ref[lax.rem(rank + k, pairs)]


def exchange(values, axis):
    return lax.all_to_all(values, axis, split_axis=0, concat_axis=0, tiled=True)


def swap(values):
    return lax.ppermute(values, "core", [(0, 1), (1, 0)])


def around(pieces, axis="sect"):
    count = len(pieces)
    arrived = list(pieces)
    for k in (2, 1, 3):
        arrived[k] = lax.ppermute(pieces[k], axis, [(i, (i + k) % count) for i in range(count)])
    return arrived


def call(kernel, name, out_shape, in_specs=None, scratch_shapes=()):
    extra = {} if in_specs is None else {"in_specs": in_specs}
    return pl.pallas_call(
        kernel,
        out_shape=out_shape,
        scratch_shapes=scratch_shapes,
        compiler_params=pltpu.CompilerParams(vmem_limit_bytes=16 << 20),
        name=name,
        **extra,
    )


def per_device(
    queries,
    key_cache,
    cached_values,
    incoming_keys,
    incoming_values,
    lengths,
    residual,
    out_proj,
    norm_gain,
    router,
    gate_proj,
    up_proj,
    down_proj,
    routes,
):
    sections = lax.axis_size("sect")
    ranks = lax.axis_size("zhi")
    _, tokens, heads, head_size = queries.shape
    slots = key_cache.shape[3]
    width = heads * head_size
    group, columns = residual.shape
    experts = router.shape[1]
    capacity = group // 2
    features = norm_gain.shape[0]
    half = features // sections // 2
    hidden_units = gate_proj.shape[2]
    rows = experts * capacity // sections
    struct = jax.ShapeDtypeStruct
    vmem = pltpu.VMEM

    gain = norm_gain.reshape(1, features)
    operands = (
        key_cache.reshape(tokens, slots, head_size),
        jnp.swapaxes(queries[0], 0, 1),
        lengths[0],
        incoming_keys.reshape(tokens, head_size),
        routes.T,
        gain,
        router.T,
        cached_values.reshape(tokens, slots, head_size),
        incoming_values.reshape(tokens, head_size),
        out_proj.T,
        residual,
    )
    attended, weight, residual, side, taken = call(
        attend_kernel,
        "attend",
        [
            struct((tokens, width), bf16),
            struct((columns, features), bf16),
            struct((group, columns), bf16),
            struct((2 * experts, half), f32),
            struct((experts * capacity, group), bf16),
        ],
        [pl.BlockSpec(memory_space=pltpu.HBM)] * len(operands),
        [
            pltpu.SMEM((tokens,), jnp.int32),
            vmem((heads, tokens, head_size), bf16),
            vmem((tokens, slots, head_size), bf16),
            vmem((tokens, slots, head_size), bf16),
            vmem((tokens, head_size), bf16),
            vmem((tokens, head_size), bf16),
            vmem((2, group), jnp.int32),
            vmem((1, features), f32),
            vmem((experts, features), bf16),
            pltpu.SemaphoreType.DMA((len(operands),)),
        ],
    )(*(pltpu.with_memory_space_constraint(operand, pltpu.HBM) for operand in operands))
    own = around([jnp.stack(around([attended] * ranks, "zhi"))] * sections)
    other = [swap(own[0]), swap(jnp.stack(own[1:]))]
    total = call(project_own_kernel, "project_own", struct((group, columns), f32))(*own, weight)
    hidden = call(project_kernel, "project", struct((group, columns), bf16))(
        *other, total, weight, residual
    )

    outgoing, stats = call(
        dispatch_kernel,
        "dispatch",
        [struct((experts, capacity, half), bf16), struct((group, 128), f32)],
        None,
        [vmem((ranks, group, columns), bf16), vmem((group, half), f32)],
    )(*around([hidden] * ranks, "zhi"), side, taken)
    other_stats = swap(stats)
    arrived = exchange(outgoing, "dp")
    expand_operands = (arrived, swap(arrived), stats, other_stats, gain, gate_proj[0], up_proj[0])

    def expand(name, offsets):
        def kernel(*refs):
            expand_kernel(*refs, offsets=offsets)

        count = len(offsets) * rows
        return call(
            kernel,
            name,
            [struct((rows, 2 * hidden_units + 128), bf16)] * len(offsets),
            None,
            [vmem((count, 2 * half), f32), vmem((count, 2 * half), bf16)],
        )(*expand_operands)

    def outward(values, by):
        pairs = []
        for i in range(sections):
            pairs += [(2 * i, 2 * ((i + by) % sections)), (2 * i + 1, 2 * ((i - by) % sections) + 1)]
        return lax.ppermute(values, ("sect", "core"), pairs)

    (far,) = expand("expand_far", ((2, 2),))
    far = outward(far, 1)
    kept, direct, passed = expand("expand_near", ((0, 0), (3, 1), (1, 3)))
    direct = outward(direct, -1)
    passed = call(relay_kernel, "relay", struct((rows, 2 * hidden_units + 128), bf16))(passed, far)

    def activate(*refs):
        activate_kernel(*refs, features=features, capacity=capacity)

    activated, combine = call(
        activate,
        "activate",
        [struct((rows, hidden_units), bf16), struct((group, experts * capacity), f32)],
    )(kept, direct, outward(passed, 1), routes.T)

    keep, give = call(
        contract_kernel,
        "contract",
        [struct((experts, capacity, half), f32), struct((experts, capacity, half), bf16)],
        None,
        [vmem((sections, rows, hidden_units), bf16), vmem((experts * capacity, half), f32)],
    )(*around([activated] * sections), down_proj[0])
    outputs = (keep + swap(give).astype(f32)).astype(bf16)

    mixed = call(
        combine_kernel,
        "combine",
        [struct((group, columns), bf16)] * ranks,
        None,
        [vmem((group, half), f32), vmem((ranks, group, columns), bf16)],
    )(exchange(outputs, "dp"), combine)
    total = hidden.astype(f32)
    for part in around(mixed, "zhi"):
        total = total + part.astype(f32)
    return total.astype(bf16)


def solution(mesh):
    sections, blocks, ranks = (mesh.shape[axis] for axis in ("sect", "dp", "tp"))
    devices = mesh.devices.reshape(sections, blocks, ranks // 2, 2)
    fine = Mesh(devices, ("sect", "dp", "zhi", "core"))
    tp = ("zhi", "core")
    placed = (
        P("dp", "sect", tp, None),
        P("dp", "sect", tp, None, None),
        P("dp", "sect", tp, None, None),
        P("dp", "sect", tp, None),
        P("dp", "sect", tp, None),
        P("dp", "sect"),
        P("dp", ("sect",) + tp),
        P(None, ("sect",) + tp),
        P(),
        P(),
        P("dp", "sect", tp),
        P("dp", "sect", tp),
        P("dp", tp, "sect"),
        P("dp", None),
    )
    return jax.shard_map(
        per_device, mesh=fine, in_specs=placed, out_specs=P("dp", ("sect",) + tp), check_vma=False
    )
```

```python
import math

import jax
import jax.numpy as jnp
from jax import lax
from jax.experimental import pallas as pl
from jax.experimental.pallas import tpu as pltpu
from jax.sharding import Mesh
from jax.sharding import PartitionSpec as P

norm_epsilon = 1e-05
f32 = jnp.float32
bf16 = jnp.bfloat16
last_with_last = (((1,), (1,)), ((), ()))
LOW = 16
SLOT = 32
FAR = 64


def lane_pick(values, lane):
    at = lax.broadcasted_iota(jnp.int32, values.shape, 1)
    return jnp.sum(jnp.where(at == lane, values, 0.0), axis=1, keepdims=True)


def high_part(values):
    return values.astype(bf16).astype(f32)


def place(routes_ref, gain_ref, router_ref, side_ref, taken_ref):
    experts = router_ref.shape[0]
    half = side_ref.shape[1]
    width = half // 4
    share = 2 * half
    slots, tokens = taken_ref.shape
    capacity = slots // experts
    first = lax.axis_index("core") == 0
    at = pl.multiple_of(lax.axis_index("sect") * share, 128)
    gain = gain_ref[:, pl.ds(at, share)]
    router = router_ref[:, pl.ds(at, share)].astype(f32)
    for pair in range(4):
        here = slice(pair * width, (pair + 1) * width)
        even = slice(2 * pair * width, (2 * pair + 1) * width)
        odd = slice((2 * pair + 1) * width, (2 * pair + 2) * width)
        side_ref[0:experts, here] = jnp.where(first, router[:, even], router[:, odd])
        side_ref[experts : experts + 1, here] = jnp.where(first, gain[:, even], gain[:, odd])
    routes = routes_ref[...]
    expert = lax.broadcasted_iota(jnp.int32, (experts, tokens), 0)
    named = [jnp.where(expert == routes[k : k + 1], 1.0, 0.0) for k in range(2)]
    before = jnp.where(
        lax.broadcasted_iota(jnp.int32, (tokens, tokens), 0)
        < lax.broadcasted_iota(jnp.int32, (tokens, tokens), 1),
        1.0,
        0.0,
    )
    earlier = jnp.dot(
        (named[0] + named[1]).astype(bf16), before.astype(bf16), preferred_element_type=f32
    )
    row = lax.broadcasted_iota(jnp.int32, (slots, tokens), 0)
    taken = jnp.zeros((slots, tokens), f32)
    for k in range(2):
        slot = jnp.sum(named[k] * earlier, axis=0, keepdims=True).astype(jnp.int32)
        taken = jnp.where(row == routes[k : k + 1] * capacity + slot, 1.0, taken)
    taken_ref[...] = taken.astype(bf16)


def attend_kernel(*refs):
    sources, outs, scratch = refs[:11], refs[11:16], refs[16:]
    out_ref, weight_ref, residual_ref, side_ref, taken_ref = outs
    lengths, q_ref, k_ref, v_ref, nk_ref, nv_ref, routes_ref, gain_ref, router_ref, sems = scratch
    targets = (
        k_ref,
        q_ref,
        lengths,
        nk_ref,
        routes_ref,
        gain_ref,
        router_ref,
        v_ref,
        nv_ref,
        weight_ref,
        residual_ref,
    )
    copies = [
        pltpu.make_async_copy(source, target, sems.at[i])
        for i, (source, target) in enumerate(zip(sources, targets, strict=True))
    ]
    for copy in copies:
        copy.start()
    for copy in copies[4:7]:
        copy.wait()
    place(routes_ref, gain_ref, router_ref, side_ref, taken_ref)
    for copy in copies[:4]:
        copy.wait()
    heads, tokens, head_size = q_ref.shape
    slots = k_ref.shape[1]
    rows = heads * tokens
    columns = tokens * slots
    scale = 1.0 / math.sqrt(head_size)
    queries = q_ref[...]
    scores = (
        lax.dot_general(
            queries.reshape(rows, head_size),
            k_ref[...].reshape(columns, head_size),
            last_with_last,
            preferred_element_type=f32,
        )
        * scale
    )
    column = lax.broadcasted_iota(jnp.int32, (1, columns), 1)
    owner = jnp.full((1, columns), -1, jnp.int32)
    for token in range(tokens):
        inside = (column >= token * slots) & (column < token * slots + lengths[token])
        owner = jnp.where(inside, token, owner)
    row_token = lax.broadcasted_iota(jnp.int32, (rows, 1), 0) & (tokens - 1)
    scores = jnp.where(row_token == owner, scores, -1e30)
    fresh = (
        jnp.sum(
            queries.astype(f32) * nk_ref[...].astype(f32)[None], axis=-1, keepdims=True
        ).reshape(rows, 1)
        * scale
    )
    highest = jnp.maximum(jnp.max(scores, axis=1, keepdims=True), fresh)
    weights = jnp.exp(scores - highest)
    fresh_weight = jnp.exp(fresh - highest)
    inverse = 1.0 / (jnp.sum(weights, axis=1, keepdims=True) + fresh_weight)
    probs = (weights * inverse).astype(bf16)
    fresh_prob = high_part(fresh_weight * inverse)
    for copy in copies[7:9]:
        copy.wait()
    fresh_values = jnp.broadcast_to(
        nv_ref[...].astype(f32)[None], (heads, tokens, head_size)
    ).reshape(rows, head_size)
    attended = jnp.dot(probs, v_ref[...].reshape(columns, head_size), preferred_element_type=f32)
    attended = (attended + fresh_prob * fresh_values).astype(bf16)
    for head in range(heads):
        block = attended[head * tokens : (head + 1) * tokens]
        out_ref[:, head * head_size : (head + 1) * head_size] = block
    for copy in copies[9:]:
        copy.wait()


def head_products(pieces, weight_ref, core):
    ranks, _, width = pieces[0].shape
    total = None
    for rank in range(ranks):
        rows = jnp.concatenate([piece[rank] for piece in pieces], axis=0)
        source = lax.rem(lax.axis_index("zhi") + ranks - rank, ranks)
        at = pl.multiple_of((2 * source + core) * width, 128)
        product = lax.dot_general(
            rows, weight_ref[:, pl.ds(at, width)], last_with_last, preferred_element_type=f32
        )
        total = product if total is None else total + product
    return total


def project_own_kernel(*refs):
    pieces, (weight_ref, total_ref) = refs[:4], refs[4:]
    total_ref[...] = head_products(pieces, weight_ref, lax.axis_index("core"))


def project_kernel(
    near, far, total_ref, weight_ref, residual_ref, hidden_ref, packed_ref, wide_ref, packed_wide
):
    other = [near] + [far.at[k] for k in range(3)]
    section = lax.axis_index("sect")
    tokens = near.shape[1]
    total = total_ref[...] + head_products(other, weight_ref, 1 - lax.axis_index("core"))
    for k in range(len(other)):
        at = pl.multiple_of(lax.rem(section + len(other) - k, len(other)) * tokens, tokens)
        hidden = residual_ref[pl.ds(at, tokens), :].astype(f32) + total[k * tokens : (k + 1) * tokens]
        wide_ref[pl.ds(at, tokens), :] = hidden
    hidden_ref[...] = wide_ref[...].astype(bf16)
    rows, width = packed_ref.shape[0], wide_ref.shape[1]
    packed_wide[:, :width] = wide_ref[:rows, :]
    packed_wide[:, width:] = wide_ref[rows:, :]
    packed_ref[...] = packed_wide[...].astype(bf16)


def dispatch_kernel(*refs):
    pieces, (side_ref, taken_ref, out_ref, stats_ref, half_ref, wide_ref) = refs[:4], refs[4:]
    pairs, rows, double = half_ref.shape
    width = double // 2
    experts = out_ref.shape[0]
    rank = lax.axis_index("zhi")
    for k, piece in enumerate(pieces):
        half_ref[lax.rem(rank + pairs - k, pairs)] = piece[...].astype(f32)
    for pair in range(pairs):
        here = slice(pair * width, (pair + 1) * width)
        wide_ref[:rows, here] = half_ref[pair, :, :width]
        wide_ref[rows:, here] = half_ref[pair, :, width:]
    wide = wide_ref[...]
    squares = jnp.sum(wide * wide, axis=1, keepdims=True)
    logits = lax.dot_general(
        (wide * side_ref[experts : experts + 1, :]).astype(bf16),
        side_ref[0:experts, :].astype(bf16),
        last_with_last,
        preferred_element_type=f32,
    )
    stats_ref[...] = jnp.zeros(stats_ref.shape, f32)
    stats_ref[:, :experts] = logits
    stats_ref[:, experts : experts + 1] = squares
    rows = jnp.dot(taken_ref[...], wide.astype(bf16), preferred_element_type=f32)
    out_ref[...] = rows.astype(bf16).reshape(out_ref.shape)


def expand_kernel(
    own_ref, other_ref, own_stats, other_stats, gain_ref, gate_ref, up_ref, *rest, offsets
):
    outs, wide_ref, scaled_ref = rest[:-2], rest[-2], rest[-1]
    sections = 4
    blocks, capacity, half = own_ref.shape
    per = blocks // sections
    rows = per * capacity
    share = 2 * half
    hidden_units = gate_ref.shape[1]
    pairs = 4
    width = half // pairs
    first = lax.axis_index("core") == 0
    section = lax.axis_index("sect")
    for k, offset in enumerate(offsets):
        at = lax.rem(section + jnp.where(first, offset[0], offset[1]), sections) * per
        own = own_ref[pl.ds(at, per)].astype(f32).reshape(rows, half)
        other = other_ref[pl.ds(at, per)].astype(f32).reshape(rows, half)
        for pair in range(pairs):
            mine = own[:, pair * width : (pair + 1) * width]
            theirs = other[:, pair * width : (pair + 1) * width]
            even = 2 * pair * width
            odd = even + width
            wide_ref[k * rows : (k + 1) * rows, even:odd] = jnp.where(first, mine, theirs)
            wide_ref[k * rows : (k + 1) * rows, odd : odd + width] = jnp.where(first, theirs, mine)
    gain = gain_ref[:, pl.ds(pl.multiple_of(section * share, 128), share)]
    stats = own_stats[...] + other_stats[...]
    high = high_part(stats)
    stats = high + pltpu.roll(stats - high, LOW, 1)
    lane = lax.broadcasted_iota(jnp.int32, (rows, 128), 1)
    for k in range(len(offsets)):
        x = wide_ref[k * rows : (k + 1) * rows, :]
        squares = jnp.sum(x * x, axis=1, keepdims=True)
        scaled_ref[k * rows : (k + 1) * rows, :] = (x * gain).astype(bf16)
        high = high_part(squares)
        extra = jnp.where(lane == SLOT, high, jnp.where(lane == SLOT + 1, squares - high, stats))
        outs[k][:, 2 * hidden_units :] = extra.astype(bf16)

    tile = 1024

    def step(i, carry):
        at = pl.multiple_of(i * tile, tile)
        for which, weight_ref in enumerate((gate_ref, up_ref)):
            product = jnp.dot(
                scaled_ref[...], weight_ref[:, pl.ds(at, tile)], preferred_element_type=f32
            ).astype(bf16)
            target = pl.multiple_of(which * hidden_units + i * tile, tile)
            for k in range(len(offsets)):
                outs[k][:, pl.ds(target, tile)] = product[k * rows : (k + 1) * rows]
        return carry

    lax.fori_loop(0, hidden_units // tile, step, 0)


def relay_kernel(piece_ref, far_ref, out_ref):
    total = piece_ref.shape[1]
    products = slice(0, total - 128)
    stats = slice(total - 128, total)
    out_ref[:, products] = (
        piece_ref[:, products].astype(f32) + far_ref[:, products].astype(f32)
    ).astype(bf16)
    lane = lax.broadcasted_iota(jnp.int32, (piece_ref.shape[0], 128), 1)
    extra = jnp.where(
        lane < FAR, piece_ref[:, stats].astype(f32), pltpu.roll(far_ref[:, stats].astype(f32), FAR, 1)
    )
    out_ref[:, stats] = extra.astype(bf16)


def activate_kernel(*refs, features, capacity):
    parts, (routes_ref, out_ref, combine_ref) = refs[:3], refs[3:]
    tokens, hidden_units = out_ref.shape

    def summed(start, size):
        first, second, third = (part[:, start : start + size].astype(f32) for part in parts)
        return first + second + third

    stats = summed(2 * hidden_units, 128)
    stats = stats + pltpu.roll(stats, 128 - FAR, 1)
    slot_squares = lane_pick(stats, SLOT) + lane_pick(stats, SLOT + 1)
    slot_scale = lax.rsqrt(slot_squares * (1.0 / features) + norm_epsilon)
    gate = summed(0, hidden_units) * slot_scale
    up = summed(hidden_units, hidden_units) * slot_scale
    out_ref[...] = (gate / (1.0 + jnp.exp(-gate)) * up).astype(bf16)

    experts = combine_ref.shape[1] // capacity
    lane = lax.broadcasted_iota(jnp.int32, (tokens, 128), 1)
    full = stats + pltpu.roll(stats, 128 - LOW, 1)
    token_scale = lax.rsqrt(lane_pick(full, experts) * (1.0 / features) + norm_epsilon)
    at_row = lax.broadcasted_iota(jnp.int32, (tokens, tokens), 0)
    at_lane = lax.broadcasted_iota(jnp.int32, (tokens, tokens), 1)
    before = jnp.where(at_lane < at_row, 1.0, 0.0)
    route = [
        jnp.sum(
            jnp.where(at_row == at_lane, routes_ref[k : k + 1, :].astype(f32), 0.0),
            axis=1,
            keepdims=True,
        ).astype(jnp.int32)
        for k in range(2)
    ]
    named = [jnp.where(lane == route[k], 1.0, 0.0) for k in range(2)]
    earlier = jnp.dot(
        before.astype(bf16), (named[0] + named[1]).astype(bf16), preferred_element_type=f32
    )
    chosen = [jnp.sum(named[k] * full, axis=1, keepdims=True) * token_scale for k in range(2)]
    column = lax.broadcasted_iota(jnp.int32, combine_ref.shape, 1)
    combine = jnp.zeros(combine_ref.shape, f32)
    for k in range(2):
        slot = jnp.sum(named[k] * earlier, axis=1, keepdims=True).astype(jnp.int32)
        mixing = 1.0 / (1.0 + jnp.exp(chosen[1 - k] - chosen[k]))
        combine = jnp.where(column == route[k] * capacity + slot, mixing, combine)
    combine_ref[...] = combine


def contract_kernel(a0_ref, a1_ref, a2_ref, a3_ref, weight_ref, keep_ref, give_ref, rows_ref, give_wide):
    pieces = (a0_ref, a1_ref, a2_ref, a3_ref)
    rows = a0_ref.shape[0]
    blocks, capacity, half = keep_ref.shape
    pairs = 4
    width = half // pairs
    first = lax.axis_index("core") == 0
    section = lax.axis_index("sect")
    for k, piece in enumerate(pieces):
        rows_ref[lax.rem(section + len(pieces) - k, len(pieces))] = piece[...]
    full = rows_ref[...].reshape(len(pieces) * rows, rows_ref.shape[2])
    product = jnp.dot(full, weight_ref[...], preferred_element_type=f32)
    for pair in range(pairs):
        even = product[:, 2 * pair * width : (2 * pair + 1) * width]
        odd = product[:, (2 * pair + 1) * width : (2 * pair + 2) * width]
        at = pair * width
        kept = jnp.where(first, even, odd)
        keep_ref[:, :, at : at + width] = kept.reshape(blocks, capacity, width)
        give_wide[:, at : at + width] = jnp.where(first, odd, even)
    give_ref[...] = give_wide[...].astype(bf16).reshape(give_ref.shape)


def combine_kernel(y_ref, combine_ref, *rest):
    outs, wide_ref, parts_ref = rest[:4], rest[4], rest[5]
    pairs, tokens, width = parts_ref.shape
    rank = lax.axis_index("zhi")
    y = y_ref[...].reshape(combine_ref.shape[1], y_ref.shape[2])
    combine = combine_ref[...]
    high = combine.astype(bf16)
    low = (combine - high.astype(f32)).astype(bf16)
    wide_ref[...] = jnp.dot(high, y, preferred_element_type=f32) + jnp.dot(
        low, y, preferred_element_type=f32
    )
    for pair in range(pairs):
        parts_ref[pair] = wide_ref[:, pair * width : (pair + 1) * width].astype(bf16)
    for k, out in enumerate(outs):
        out[...] = parts_ref[lax.rem(rank + k, pairs)]


def exchange(values, axis):
    return lax.all_to_all(values, axis, split_axis=0, concat_axis=0, tiled=True)


def swap(values):
    return lax.ppermute(values, "core", [(0, 1), (1, 0)])


def around(pieces, axis="sect"):
    count = len(pieces)
    arrived = list(pieces)
    for k in (2, 1, 3):
        arrived[k] = lax.ppermute(pieces[k], axis, [(i, (i + k) % count) for i in range(count)])
    return arrived


def call(kernel, name, out_shape, in_specs=None, scratch_shapes=()):
    extra = {} if in_specs is None else {"in_specs": in_specs}
    return pl.pallas_call(
        kernel,
        out_shape=out_shape,
        scratch_shapes=scratch_shapes,
        compiler_params=pltpu.CompilerParams(vmem_limit_bytes=16 << 20),
        name=name,
        **extra,
    )


def per_device(
    queries,
    key_cache,
    cached_values,
    incoming_keys,
    incoming_values,
    lengths,
    residual,
    out_proj,
    norm_gain,
    router,
    gate_proj,
    up_proj,
    down_proj,
    routes,
):
    sections = lax.axis_size("sect")
    ranks = lax.axis_size("zhi")
    _, tokens, heads, head_size = queries.shape
    slots = key_cache.shape[3]
    width = heads * head_size
    group, columns = residual.shape
    experts = router.shape[1]
    capacity = group // 2
    features = norm_gain.shape[0]
    half = features // sections // 2
    hidden_units = gate_proj.shape[2]
    rows = experts * capacity // sections
    struct = jax.ShapeDtypeStruct
    vmem = pltpu.VMEM

    gain = norm_gain.reshape(1, features)
    operands = (
        key_cache.reshape(tokens, slots, head_size),
        jnp.swapaxes(queries[0], 0, 1),
        lengths[0],
        incoming_keys.reshape(tokens, head_size),
        routes.T,
        gain,
        router.T,
        cached_values.reshape(tokens, slots, head_size),
        incoming_values.reshape(tokens, head_size),
        out_proj.T,
        residual,
    )
    attended, weight, residual, side, taken = call(
        attend_kernel,
        "attend",
        [
            struct((tokens, width), bf16),
            struct((columns, features), bf16),
            struct((group, columns), bf16),
            struct((2 * experts, half), f32),
            struct((experts * capacity, group), bf16),
        ],
        [pl.BlockSpec(memory_space=pltpu.HBM)] * len(operands),
        [
            pltpu.SMEM((tokens,), jnp.int32),
            vmem((heads, tokens, head_size), bf16),
            vmem((tokens, slots, head_size), bf16),
            vmem((tokens, slots, head_size), bf16),
            vmem((tokens, head_size), bf16),
            vmem((tokens, head_size), bf16),
            vmem((2, group), jnp.int32),
            vmem((1, features), f32),
            vmem((experts, features), bf16),
            pltpu.SemaphoreType.DMA((len(operands),)),
        ],
    )(*(pltpu.with_memory_space_constraint(operand, pltpu.HBM) for operand in operands))
    own = around([jnp.stack(around([attended] * ranks, "zhi"))] * sections)
    other = [swap(own[0]), swap(jnp.stack(own[1:]))]
    total = call(project_own_kernel, "project_own", struct((group, columns), f32))(*own, weight)
    hidden, packed = call(
        project_kernel,
        "project",
        [struct((group, columns), bf16), struct((group // 2, 2 * columns), bf16)],
        None,
        [vmem((group, columns), f32), vmem((group // 2, 2 * columns), f32)],
    )(*other, total, weight, residual)

    outgoing, stats = call(
        dispatch_kernel,
        "dispatch",
        [struct((experts, capacity, half), bf16), struct((group, 128), f32)],
        None,
        [vmem((ranks, group // 2, 2 * columns), f32), vmem((group, half), f32)],
    )(*around([packed] * ranks, "zhi"), side, taken)
    other_stats = swap(stats)
    arrived = exchange(outgoing, "dp")
    expand_operands = (arrived, swap(arrived), stats, other_stats, gain, gate_proj[0], up_proj[0])

    def expand(name, offsets):
        def kernel(*refs):
            expand_kernel(*refs, offsets=offsets)

        count = len(offsets) * rows
        return call(
            kernel,
            name,
            [struct((rows, 2 * hidden_units + 128), bf16)] * len(offsets),
            None,
            [vmem((count, 2 * half), f32), vmem((count, 2 * half), bf16)],
        )(*expand_operands)

    def outward(values, by):
        pairs = []
        for i in range(sections):
            pairs += [(2 * i, 2 * ((i + by) % sections)), (2 * i + 1, 2 * ((i - by) % sections) + 1)]
        return lax.ppermute(values, ("sect", "core"), pairs)

    (far,) = expand("expand_far", ((2, 2),))
    far = outward(far, 1)
    kept, direct, passed = expand("expand_near", ((0, 0), (3, 1), (1, 3)))
    direct = outward(direct, -1)
    passed = call(relay_kernel, "relay", struct((rows, 2 * hidden_units + 128), bf16))(passed, far)

    def activate(*refs):
        activate_kernel(*refs, features=features, capacity=capacity)

    activated, combine = call(
        activate,
        "activate",
        [struct((rows, hidden_units), bf16), struct((group, experts * capacity), f32)],
    )(kept, direct, outward(passed, 1), routes.T)

    keep, give = call(
        contract_kernel,
        "contract",
        [struct((experts, capacity, half), f32), struct((experts, capacity, half), bf16)],
        None,
        [vmem((sections, rows, hidden_units), bf16), vmem((experts * capacity, half), f32)],
    )(*around([activated] * sections), down_proj[0])
    outputs = (keep + swap(give).astype(f32)).astype(bf16)

    mixed = call(
        combine_kernel,
        "combine",
        [struct((group, columns), bf16)] * ranks,
        None,
        [vmem((group, half), f32), vmem((ranks, group, columns), bf16)],
    )(exchange(outputs, "dp"), combine)
    total = hidden.astype(f32)
    for part in around(mixed, "zhi"):
        total = total + part.astype(f32)
    return total.astype(bf16)


def solution(mesh):
    sections, blocks, ranks = (mesh.shape[axis] for axis in ("sect", "dp", "tp"))
    devices = mesh.devices.reshape(sections, blocks, ranks // 2, 2)
    fine = Mesh(devices, ("sect", "dp", "zhi", "core"))
    tp = ("zhi", "core")
    placed = (
        P("dp", "sect", tp, None),
        P("dp", "sect", tp, None, None),
        P("dp", "sect", tp, None, None),
        P("dp", "sect", tp, None),
        P("dp", "sect", tp, None),
        P("dp", "sect"),
        P("dp", ("sect",) + tp),
        P(None, ("sect",) + tp),
        P(),
        P(),
        P("dp", "sect", tp),
        P("dp", "sect", tp),
        P("dp", tp, "sect"),
        P("dp", None),
    )
    return jax.shard_map(
        per_device, mesh=fine, in_specs=placed, out_specs=P("dp", ("sect",) + tp), check_vma=False
    )
```
